32 devices in a mesh: dom: 8 (over y, x, core), col: 4 (over z).
Axes of the slice: x: 2, y: 2, z: 4, core: 2. Of those that a mesh axis runs over, the one named last changes fastest.
Arguments:
- basis_panel: bfloat16 [256, 163840], P('col', 'dom'), may hold values from -12 to 12
- jacobian: bfloat16 [2, 320, 16384], P(None, None, 'dom'), may hold values from -0.25 to 0.25
- neighbors: int32 [512, 2], P('dom'), may hold values from 0 to 63
- sample_rows: int32 [16384], P('dom'), may hold values from 0 to 8191, as said below
- residual_parts: float32 [16384], P('dom'), may hold values from -48 to 48
Outputs:
- jacobian_basis: float32 [256, 8192], P('col', 'dom')
- sampled_residual: float32 [8192], P('dom')
- reduced_step: float32 [256], P('col')
The draws below stay inside these ranges and needn't reach their ends.
Inputs may be any that keep to these rules, and one draw needn't show every extreme that they name: `sample_rows`: for each index d of dom, its 2048 entries name each of its own rows d * 1024 to d * 1024 + 1023 exactly once; the other 1024 entries name rows owned by the 7 indices d + 1 to d + 7 of dom, cyclically, at most 256 to any one of them and exactly 256 to one of them. `neighbors`: each entry is an element of the same index of dom, counted from that index's first element.
All inputs are finite; a program needn't handle non-finite values.
Results may differ from the reference program's by a relative error of at most 0.0003.
Values sent between devices are 32-bit elements; how exact they have to be, the bound alone decides.
A program may use at most 64 MiB of HBM per device.

```python
import jax
import jax.numpy as jnp
from jax import lax

K = 256
NODE = 320
NB = 2
RS = 32
E_DEV = 64
ROWS_DEV = 1024
CAP = 256
REACH = 7
N_ELEM = 512
SAMPLES = 8192
DOFS = 163840
N_DOM = 8


def rows_of_device(key, device):
    keys = jax.random.split(jax.random.fold_in(key, device), 5)
    busy_offset = jax.random.randint(keys[0], (), 1, REACH + 1)
    spread = jnp.arange(REACH - 1, dtype=jnp.int32)
    others = 1 + (busy_offset + spread) % REACH
    chosen = jax.random.permutation(keys[1], (REACH - 1) * CAP)[:ROWS_DEV - CAP]
    offsets = jnp.concatenate([jnp.zeros((ROWS_DEV,), jnp.int32), jnp.full((CAP,), busy_offset, jnp.int32), others[chosen // CAP]])
    local_rows = jnp.concatenate([jax.random.permutation(keys[2], ROWS_DEV), jax.random.randint(keys[3], (ROWS_DEV,), 0, ROWS_DEV)])
    owners = (device + offsets) % N_DOM
    mixing = jax.random.permutation(keys[4], 2 * ROWS_DEV)
    return (owners * ROWS_DEV + local_rows)[mixing].astype(jnp.int32)


def draw_sample_rows(key, part):
    devices = jnp.arange(N_DOM, dtype=jnp.int32)
    return jax.vmap(lambda device: rows_of_device(key, device))(devices).reshape(-1)


def draw_basis_panel(key, part):
    keys = jax.random.split(key, 3)
    noise = jax.random.truncated_normal(keys[0], -5.0, 5.0, (K, DOFS), jnp.float32)
    weights = jax.random.uniform(keys[1], (K, 1), jnp.float32, 0.5, 1.5)
    shared = jax.random.truncated_normal(keys[2], -5.0, 5.0, (1, DOFS), jnp.float32)
    return (noise + 0.6 * weights * shared).astype(jnp.bfloat16)


def set_ends(result, rng, least, high):
    longest = result.shape.index(max(result.shape))
    spots = []
    for shift in (0, 1):
        where = [jax.random.randint(jax.random.fold_in(rng, axis), (), 0, length) for axis, length in enumerate(result.shape)]
        where[longest] = (where[longest] + shift) % result.shape[longest]
        spots.append(tuple(where))
    return result.at[spots[0]].set(least).at[spots[1]].set(high)


def shard_levels(rng, extent, shards, low, high):
    loudness, own = 1.0, jax.random.fold_in(rng, 6)
    for position, blocks in shards:
        steps = jnp.exp(jax.random.uniform(jax.random.fold_in(own, position), (blocks,), jnp.float32, low / len(shards), high / len(shards)))
        loudness = loudness * jnp.repeat(steps, extent[position] // blocks).reshape([-1 if axis == position else 1 for axis in range(len(extent))])
    return loudness


def scatter_about(rng, extent, width, limit, cuts=(), kind=jnp.bfloat16):
    drawn = jax.random.normal(rng, extent, jnp.float32) * width
    if len(cuts) > 0:
        drawn = shard_levels(rng, extent, cuts, -0.22, 0.18) * drawn
    return jnp.clip(drawn, min=-limit, max=limit).astype(kind)


def setup_inputs(seed: int = 0) -> dict:
    streams_of = jax.random.split(jax.random.key(seed), 6)
    return {
        "basis_panel": draw_basis_panel(jax.random.fold_in(streams_of[5], 71), 0),
        "jacobian": scatter_about(streams_of[1], (NB, NODE, N_ELEM * RS), (NB * NODE) ** -0.5, 0.25, ((2, 8),)),
        "neighbors": set_ends(jax.random.randint(streams_of[2], (N_ELEM, NB), 0, E_DEV), jax.random.fold_in(streams_of[2], 1), 0, E_DEV - 1).astype(jnp.int32),
        "sample_rows": draw_sample_rows(jax.random.fold_in(streams_of[5], 71), 0),
        "residual_parts": scatter_about(streams_of[4], (N_ELEM * RS,), 8.0, 48.0, ((0, 8),), jnp.float32),
    }


def reference(basis_panel, jacobian, neighbors, sample_rows, residual_parts):
    panels = basis_panel.reshape(K, N_DOM, E_DEV, NODE).transpose(1, 0, 2, 3)
    blocks = jacobian.reshape(NB, NODE, N_DOM, E_DEV, RS).transpose(2, 0, 1, 3, 4)
    links = neighbors.reshape(N_DOM, E_DEV, NB)

    def per_device(operands):
        panel_slab, block_slab, link_slab = operands
        summed = jnp.zeros((K, E_DEV, RS), jnp.float32)
        for coupled in range(NB):
            picked = jnp.take(panel_slab, link_slab[:, coupled], axis=1).astype(jnp.float32)
            summed = summed + jnp.einsum('cep,per->cer', picked, block_slab[coupled].astype(jnp.float32), precision=lax.Precision.HIGHEST)
        return summed.reshape(K, E_DEV * RS)
    partial_value = lax.map(per_device, (panels, blocks, links))
    partial_value = partial_value.transpose(1, 0, 2).reshape(K, N_ELEM * RS)
    jacobian_basis = jnp.zeros((K, SAMPLES), jnp.float32).at[:, sample_rows].add(partial_value)
    sampled_residual = jnp.zeros((SAMPLES,), jnp.float32).at[sample_rows].add(residual_parts)
    gram_matrix = jnp.einsum('kr,lr->kl', jacobian_basis, jacobian_basis, precision=lax.Precision.HIGHEST)
    gradient = jnp.einsum('kr,r->k', jacobian_basis, sampled_residual, precision=lax.Precision.HIGHEST)
    factor = jnp.linalg.cholesky(gram_matrix)
    forward = lax.linalg.triangular_solve(factor, gradient[:, None], left_side=True, lower=True)
    backward = lax.linalg.triangular_solve(factor, forward, left_side=True, lower=True, transpose_a=True)
    reduced_step = -backward[:, 0]
    return (jacobian_basis, sampled_residual, reduced_step)
```

```python
import functools

import jax
import jax.numpy as jnp
from jax import lax
from jax.experimental import pallas as pl
from jax.experimental.pallas import tpu as pltpu
from jax.sharding import PartitionSpec as P

ROWS_DEV = 1024
CAP = 256
REACH_MOST = 8
LANES = 128
PIVOTS = 16
HIGHEST = lax.Precision.HIGHEST
F32 = jnp.float32
BF16 = jnp.bfloat16


def iota(shape, dim):
    return lax.broadcasted_iota(jnp.int32, shape, dim)


def dot_nn(a, b, precision=None):
    return lax.dot_general(
        a, b, (((1,), (0,)), ((), ())), precision=precision, preferred_element_type=F32
    )


def dot_nt(a, b, precision=None):
    return lax.dot_general(
        a, b, (((1,), (1,)), ((), ())), precision=precision, preferred_element_type=F32
    )


def dot_tn(a, b, precision=None):
    return lax.dot_general(
        a, b, (((0,), (0,)), ((), ())), precision=precision, preferred_element_type=F32
    )


def split_values(x):
    high = x.astype(BF16)
    return high, (x - high.astype(F32)).astype(BF16)


def split_extra(x):
    high = x.astype(BF16).astype(F32)
    middle = (x - high).astype(BF16).astype(F32)
    low = x - high - middle
    return jnp.concatenate([high, middle, low, jnp.zeros_like(x)], axis=0).astype(BF16)


def join(found, width):
    values = found[:width] + found[width : 2 * width]
    base = 2 * width
    extra = found[base : base + 8] + found[base + 8 : base + 16] + found[base + 16 : base + 24]
    return jnp.concatenate([values, extra], axis=0)


def pick(terms, targets, base):
    spots = iota((CAP, targets.shape[1]), 0) + base
    return dot_nt(terms, (spots == targets).astype(F32).astype(BF16))


def fold(value, count):
    return jnp.where(value >= count, value - count, value)


def step_kernel(
    dom_count, col_count, reach, links_ref, panel_hbm, blocks_hbm, rows_ref, parts_ref,
    basis_ref, residual_ref, gram_ref,
    panel_ref, blocks_ref, load_sems, panels, terms, send, arrived, local, terms_in, landing, pieces, others, parts, paired, team_parts,
    sums, total, whole, dom_sems, col_sems, pair_sems, sum_sems, all_sems, relay_sems,
):
    dom, col = lax.axis_index("dom"), lax.axis_index("col")
    devices = dom_count * col_count
    me = dom * col_count + col
    width = panel_ref.shape[0]
    coupled_count, node, entries = blocks_ref.shape
    elements = links_ref.shape[1]
    rs = entries // elements
    group = LANES // rs
    part = ROWS_DEV // col_count
    size = width * col_count

    def remote(source, target, sems, index, device):
        return pltpu.make_async_remote_copy(
            src_ref=source,
            dst_ref=target,
            send_sem=sems.at[0, index],
            recv_sem=sems.at[1, index],
            device_id=device,
            device_id_type=pl.DeviceIdType.MESH,
        )

    def device_at(offset):
        index = fold(me + offset, devices)
        return index, (index // col_count, index % col_count)

    side, mate = dom % 2, (dom // 2 * 2 + 1 - dom % 2, col)
    team, spot = devices // 2, dom // 2 * col_count + col

    def mate_at(offset):
        index = fold(spot + offset, team)
        return index, (index // col_count * 2 + side, index % col_count)

    def dom_copy(o):
        return remote(send.at[o - 1], arrived.at[o - 1], dom_sems, o - 1, (fold(dom + o, dom_count), col))

    def col_copy(o):
        there = fold(col + o, col_count)
        return remote(pieces.at[there], others.at[col], col_sems, o - 1, (dom, there))

    def pair_copy():
        return remote(parts.at[1 - side], paired, pair_sems, 0, mate)

    def sum_copy(o):
        index, device = mate_at(o)
        return remote(team_parts.at[index], sums.at[o - 1], sum_sems, o - 1, device)

    def all_copy(o):
        _, device = mate_at(o)
        return remote(total, whole.at[side, spot], all_sems, o - 1, device)

    def relay_copy(o):
        place = whole.at[side, fold(spot - o + team, team)]
        return remote(place, place, relay_sems, o, mate)

    panel_load = pltpu.make_async_copy(panel_hbm, panel_ref, load_sems.at[0])
    blocks_load = pltpu.make_async_copy(blocks_hbm, blocks_ref, load_sems.at[1])
    panel_load.start()
    blocks_load.start()
    barrier = pltpu.get_barrier_semaphore()

    @pl.loop(1, devices)
    def _(o):
        _, device = device_at(o)
        pl.semaphore_signal(barrier, inc=1, device_id=device, device_id_type=pl.DeviceIdType.MESH)

    shift = ROWS_DEV.bit_length() - 1
    match_rows = max(16, dom_count)
    before = (iota((LANES, LANES), 0) < iota((LANES, LANES), 1)).astype(F32).astype(BF16)
    carry = jnp.zeros((match_rows, 1), F32)
    targets = []
    for start in range(0, entries, LANES):
        rows = rows_ref[:, start : start + LANES]
        offset = fold((rows >> shift) - dom + dom_count, dom_count)
        local_row = rows & (ROWS_DEV - 1)
        matches = (iota((match_rows, LANES), 0) == offset).astype(F32)
        ranks = jnp.sum(
            matches * (dot_nn(matches.astype(BF16), before) + carry), axis=0, keepdims=True
        ).astype(jnp.int32)
        carry = carry + jnp.sum(matches, axis=1, keepdims=True)
        targets.append(
            jnp.where(offset == 0, local_row, ROWS_DEV + (offset - 1) * CAP + ranks)
        )
    targets = jnp.concatenate(targets, axis=1)

    row_values = (rows_ref[...] & (ROWS_DEV - 1)).astype(F32)
    which = iota((8, entries), 0)
    extra = jnp.where(which == 0, parts_ref[...], jnp.where(which == 1, row_values, 0.0))
    terms[2 * width :, :] = split_extra(extra)

    panel_load.wait()

    @pl.loop(0, elements // 2, unroll=4)
    def _(pair):
        window = panel_ref[:, pl.ds(pl.multiple_of(pair * 2 * node, LANES), 2 * node)]
        panels[2 * pair] = window[:, :node]
        panels[2 * pair + 1] = window[:, node:]

    lane_element = iota((width, LANES), 1) // rs

    blocks_load.wait()

    @pl.loop(0, elements // group, unroll=4)
    def _(block):
        columns = pl.ds(pl.multiple_of(block * LANES, LANES), LANES)
        found = jnp.zeros((group * width, LANES), F32)
        for coupled in range(coupled_count):
            picked = jnp.concatenate(
                [panels[links_ref[coupled, block * group + q]] for q in range(group)], axis=0
            )
            found = found + dot_nn(picked, blocks_ref[coupled, :, columns])
        out = found[:width]
        for q in range(1, group):
            out = jnp.where(lane_element == q, found[q * width : (q + 1) * width], out)
        high, low = split_values(out)
        terms[:width, columns] = high
        terms[width : 2 * width, columns] = low

    pl.semaphore_wait(barrier, devices - 1)

    @pl.loop(1, reach + 1)
    def _(o):
        send[o - 1] = join(pick(terms[...], targets, ROWS_DEV + (o - 1) * CAP), width)
        dom_copy(o).start()

    @pl.loop(0, ROWS_DEV // CAP)
    def _(tile):
        base = tile * CAP
        local[:, pl.ds(pl.multiple_of(base, CAP), CAP)] = join(
            pick(terms[...], targets, base), width
        )

    for o in range(1, reach + 1):
        dom_copy(o).wait_recv()
        columns = slice((o - 1) * CAP, o * CAP)
        high, low = split_values(arrived[o - 1, :width, :])
        terms_in[:width, columns] = high
        terms_in[width : 2 * width, columns] = low
        extra = arrived[o - 1, width:, :]
        terms_in[2 * width :, columns] = split_extra(extra)
        landing[:, columns] = extra[1:2, :].astype(jnp.int32)
    targets = landing[...]

    def assemble(base):
        columns = pl.ds(pl.multiple_of(base, CAP), CAP)
        found = join(pick(terms_in[...], targets, base), width) + local[:, columns]
        basis_ref[:, columns] = found[:width]
        residual_ref[:, columns] = found[width : width + 1]
        return found

    if part == CAP:

        @pl.loop(1, col_count)
        def _(o):
            there = fold(col + o, col_count)
            pieces[there] = assemble(there * part)[:width]
            col_copy(o).start()

        found = assemble(col * part)
        others[col] = found[:width]
        own_residual = found[width : width + 1]
    else:
        for tile in range(ROWS_DEV // CAP):
            assemble(tile * CAP)
        own_residual = jnp.zeros((1, part), F32)
        for index in range(col_count):
            columns = slice(index * part, (index + 1) * part)
            pieces[index] = basis_ref[:, columns]
            own_residual = own_residual + jnp.where(index == col, residual_ref[:, columns], 0.0)
        for o in range(1, col_count):
            col_copy(o).start()
        others[col] = pieces[col]
    for o in range(1, col_count):
        col_copy(o).wait_recv()

    basis = others[...].reshape(size, part)
    gram = dot_nt(basis, basis, HIGHEST)
    gradient = dot_nt(jnp.broadcast_to(own_residual, (8, part)), basis, HIGHEST)[:1]
    row, column = iota((size, size), 0), iota((size, size), 1)
    gram = jnp.where((row == size - 1) & (column < size - 1), gradient, gram)
    turned = pltpu.roll(jnp.broadcast_to(gradient, (8, size)), 1, axis=1)[:1]
    gram = jnp.where((row == size - 2) & (column == 0), turned, gram)
    _, count, height, span = parts.shape
    for half in range(2):
        for index in range(count):
            if span == size:
                start = (half * count + index) * height
                parts[half, index] = gram[start : start + height]
            else:
                start = (half * count + index) * span
                lane = start % size
                parts[half, index] = gram[start // size][None, lane : lane + span]
    pair_copy().start()
    pair_copy().wait_recv()
    team_parts[...] = parts[side] + paired[...]

    @pl.loop(1, team)
    def _(o):
        sum_copy(o).start()

    @pl.loop(1, team)
    def _(o):
        sum_copy(o).wait_recv()

    mine = jnp.sum(sums[...], axis=0) + team_parts[spot]
    total[...] = mine

    @pl.loop(1, team)
    def _(o):
        all_copy(o).start()

    whole[side, spot] = mine
    relay_copy(0).start()

    @pl.loop(1, team)
    def _(o):
        all_copy(o).wait_recv()
        relay_copy(o).start()

    @pl.loop(0, team)
    def _(o):
        back = whole.at[1 - side, fold(spot - o + team, team)]
        remote(back, back, relay_sems, o, mate).wait_recv()

    gram_ref[...] = whole[...]
    for o in range(1, reach + 1):
        dom_copy(o).wait_send()
    for o in range(1, col_count):
        col_copy(o).wait_send()

    pair_copy().wait_send()

    @pl.loop(1, team)
    def _(o):
        sum_copy(o).wait_send()
        all_copy(o).wait_send()

    @pl.loop(0, team)
    def _(o):
        relay_copy(o).wait_send()


def tree_sum(terms):
    while len(terms) > 1:
        odd = [terms[-1]] if len(terms) % 2 else []
        terms = [a + b for a, b in zip(terms[::2], terms[1::2])] + odd
    return terms[0]


def split_three(x):
    high = x.astype(BF16)
    rest = x - high.astype(F32)
    middle = rest.astype(BF16)
    return high, middle, (rest - middle.astype(F32)).astype(BF16)


def product(a, b):
    ah, am, al = split_three(a)
    bh, bm, bl = split_three(b)

    def pair(a1, b1, a2, b2):
        return dot_nn(
            jnp.concatenate([a1, a2], axis=1), jnp.concatenate([b1, b2], axis=0)
        )

    return pair(ah, bh, am, bh) + (pair(ah, bm, am, bm) + pair(ah, bl, al, bh))


def eliminate(matrix, side):
    size = matrix.shape[0]
    shape = (8, size)
    row, lane = iota(shape, 0), iota(shape, 1)
    tall = PIVOTS // 8
    wide = [matrix, side]
    groups = [[w[k : k + 8] for w in wide] for k in range(0, size, 8)]

    def column(x, k):
        return jnp.broadcast_to(x[:, k : k + 1], shape)

    def across(x, r):
        return jnp.broadcast_to(x[r : r + 1], shape)

    for start in range(0, size, PIVOTS):
        first = start // 8
        last = first + tall
        inside = (lane >= start) & (lane < start + PIVOTS)

        def kept(g):
            return [jnp.where(inside, 0.0, groups[g][0])] + groups[g][1:]

        panel = groups[first:last]
        columns = [[column(p[0], start + j) for j in range(PIVOTS)] for p in panel]
        work = [
            [jnp.where(inside, (lane - start - 8 * t == row).astype(F32), p[0])] + p[1:]
            for t, p in enumerate(panel)
        ]
        scales = [None] * tall
        for i in range(PIVOTS):
            own, r = divmod(i, 8)
            here = row == r
            scale = 1.0 / across(columns[own][i], r)
            factors = [columns[t][i] * scale for t in range(tall)]
            factors[own] = jnp.where(here, 0.0, factors[own])
            scales[own] = scale if r == 0 else jnp.where(here, scale, scales[own])
            for j in range(i + 1, PIVOTS):
                moved = across(columns[own][j], r)
                for t in range(tall):
                    columns[t][j] = columns[t][j] - factors[t] * moved
            for w in range(len(wide)):
                moved = across(work[own][w], r)
                for t in range(tall):
                    work[t][w] = work[t][w] - factors[t] * moved
        done = [[x * scales[t] for x in work[t]] for t in range(tall)]
        ahead = {}
        for g in range(last, min(last + tall, len(groups))):
            cols = [column(groups[g][0], start + k) for k in range(PIVOTS)]
            ahead[g] = [
                x - tree_sum([cols[k] * across(done[k // 8][w], k % 8) for k in range(PIVOTS)])
                for w, x in enumerate(kept(g))
            ]
        left = jnp.concatenate([jnp.where(inside, g[0], 0.0) for g in groups], axis=0)
        empty = [jnp.zeros(shape, F32)] * len(wide)
        right = jnp.concatenate(
            [
                jnp.concatenate(done[g - first] if first <= g < last else empty, axis=1)
                for g in range(len(groups))
            ],
            axis=0,
        )
        change = product(left, right)
        for g in range(len(groups)):
            if first <= g < last:
                groups[g] = done[g - first]
            elif g in ahead:
                groups[g] = ahead[g]
            else:
                rows = change[8 * g : 8 * g + 8]
                groups[g] = [
                    x - rows[:, size * w : size * (w + 1)] for w, x in enumerate(kept(g))
                ]
    return [jnp.concatenate([g[w] for g in groups], axis=0) for w in range(len(wide))]


def solve_kernel(
    col_ref, gram_ref, basis_ref, residual_ref, out_ref, basis_out_ref, residual_out_ref
):
    basis_out_ref[...] = basis_ref[...]
    residual_out_ref[...] = residual_ref[...]
    size = gram_ref.shape[0]
    half = size // 2
    row, column = iota((half, half), 0), iota((half, half), 1)
    upper = row <= column

    def mirrored(block):
        block = jnp.where(upper, block, 0.0)
        return block + jnp.where(row == column, 0.0, block).T

    lane = iota((1, size), 1)
    last = jnp.sum(
        jnp.where(lane == 0, gram_ref[size - 2 : size - 1, :], 0.0), axis=1, keepdims=True
    )
    gradient = jnp.where(lane == size - 1, last, gram_ref[size - 1 : size, :])
    cross = gram_ref[:half, half:]
    first_inverse, carried = eliminate(mirrored(gram_ref[:half, :half]), cross)
    second = mirrored(gram_ref[half:, half:]) - dot_tn(cross, carried, HIGHEST)
    top = jnp.broadcast_to(gradient[:, :half], (8, half))
    x_top = dot_nn(top, first_inverse, HIGHEST)[:1]
    low = gradient[:, half:] - dot_nn(top, carried, HIGHEST)[:1]
    low = jnp.broadcast_to(low, (half, half)).T
    second_inverse, back = eliminate(second, -carried.T)
    x_bottom = jnp.sum(low * second_inverse, axis=0, keepdims=True)
    x_top = x_top + jnp.sum(low * back, axis=0, keepdims=True)
    full = -jnp.concatenate([x_top, x_bottom], axis=1)
    width = out_ref.shape[1]
    out = jnp.zeros((1, width), F32)
    for index in range(size // width):
        out = jnp.where(col_ref[0] == index, full[:, index * width : (index + 1) * width], out)
    out_ref[...] = out


VMEM = pl.BlockSpec(memory_space=pltpu.VMEM)
SMEM = pl.BlockSpec(memory_space=pltpu.SMEM)
ANY = pl.BlockSpec(memory_space=pl.ANY)


def body(basis_panel, jacobian, neighbors, sample_rows, residual_parts):
    dom_count, col_count = lax.axis_size("dom"), lax.axis_size("col")
    col_index = lax.axis_index("col")
    width = basis_panel.shape[0]
    entries = sample_rows.shape[0]
    elements = neighbors.shape[0]
    node = jacobian.shape[1]
    size = width * col_count
    shape = jax.ShapeDtypeStruct
    reach = min(dom_count - 1, REACH_MOST)
    part = ROWS_DEV // col_count
    devices = dom_count * col_count
    team = devices // 2
    if size % devices == 0:
        chunk = (2, team, size // devices, size)
    else:
        chunk = (2, team, 1, size * size // devices)
    jacobian_basis, sampled_residual, whole = pl.pallas_call(
        functools.partial(step_kernel, dom_count, col_count, reach),
        out_shape=(
            shape((width, ROWS_DEV), F32), shape((1, ROWS_DEV), F32), shape(chunk, F32)
        ),
        in_specs=[SMEM, ANY, ANY, VMEM, VMEM],
        out_specs=(VMEM, VMEM, VMEM),
        scratch_shapes=[
            pltpu.VMEM(basis_panel.shape, BF16),
            pltpu.VMEM(jacobian.shape, BF16),
            pltpu.SemaphoreType.DMA((2,)),
            pltpu.VMEM((elements, width, node), BF16),
            pltpu.VMEM((2 * width + 32, entries), BF16),
            pltpu.VMEM((reach, width + 8, CAP), F32),
            pltpu.VMEM((reach, width + 8, CAP), F32),
            pltpu.VMEM((width + 8, ROWS_DEV), F32),
            pltpu.VMEM((2 * width + 32, reach * CAP), BF16),
            pltpu.VMEM((1, reach * CAP), jnp.int32),
            pltpu.VMEM((col_count, width, part), F32),
            pltpu.VMEM((col_count, width, part), F32),
            pltpu.VMEM(chunk, F32),
            pltpu.VMEM(chunk[1:], F32),
            pltpu.VMEM(chunk[1:], F32),
            pltpu.VMEM((team - 1,) + chunk[2:], F32),
            pltpu.VMEM(chunk[2:], F32),
            pltpu.VMEM(chunk, F32),
            pltpu.SemaphoreType.DMA((2, reach)),
            pltpu.SemaphoreType.DMA((2, col_count - 1)),
            pltpu.SemaphoreType.DMA((2, 1)),
            pltpu.SemaphoreType.DMA((2, team - 1)),
            pltpu.SemaphoreType.DMA((2, team - 1)),
            pltpu.SemaphoreType.DMA((2, team)),
        ],
        compiler_params=pltpu.CompilerParams(collective_id=0, has_side_effects=True),
        name="step",
    )(
        neighbors.T,
        basis_panel,
        jacobian,
        sample_rows.reshape(1, entries),
        residual_parts.reshape(1, entries),
    )
    reduced_step, jacobian_basis, sampled_residual = pl.pallas_call(
        solve_kernel,
        out_shape=(
            shape((1, width), F32), shape((width, ROWS_DEV), F32), shape((1, ROWS_DEV), F32)
        ),
        in_specs=[SMEM, VMEM, VMEM, VMEM],
        out_specs=(VMEM, VMEM, VMEM),
        name="solve",
    )(
        col_index.astype(jnp.int32).reshape(1),
        whole.reshape(size, size),
        jacobian_basis,
        sampled_residual,
    )
    return (jacobian_basis, sampled_residual[0], reduced_step[0])


def solution(mesh):
    placed = (P("col", "dom"), P(None, None, "dom"), P("dom", None), P("dom"), P("dom"))
    return jax.shard_map(
        body,
        mesh=mesh,
        in_specs=placed,
        out_specs=(P("col", "dom"), P("dom"), P("col")),
        check_vma=False,
    )
```

```python
import functools

import jax
import jax.numpy as jnp
from jax import lax
from jax.experimental import pallas as pl
from jax.experimental.pallas import tpu as pltpu
from jax.sharding import PartitionSpec as P

ROWS_DEV = 1024
CAP = 256
REACH_MOST = 8
LANES = 128
PIVOTS = 16
HIGHEST = lax.Precision.HIGHEST
F32 = jnp.float32
BF16 = jnp.bfloat16


def iota(shape, dim):
    return lax.broadcasted_iota(jnp.int32, shape, dim)


def dot_nn(a, b, precision=None):
    return lax.dot_general(
        a, b, (((1,), (0,)), ((), ())), precision=precision, preferred_element_type=F32
    )


def dot_nt(a, b, precision=None):
    return lax.dot_general(
        a, b, (((1,), (1,)), ((), ())), precision=precision, preferred_element_type=F32
    )


def dot_tn(a, b, precision=None):
    return lax.dot_general(
        a, b, (((0,), (0,)), ((), ())), precision=precision, preferred_element_type=F32
    )


def split_values(x):
    high = x.astype(BF16)
    return high, (x - high.astype(F32)).astype(BF16)


def split_extra(x):
    high = x.astype(BF16).astype(F32)
    middle = (x - high).astype(BF16).astype(F32)
    low = x - high - middle
    return jnp.concatenate([high, middle, low, jnp.zeros_like(x)], axis=0).astype(BF16)


def join(found, width):
    values = found[:width] + found[width : 2 * width]
    base = 2 * width
    extra = found[base : base + 8] + found[base + 8 : base + 16] + found[base + 16 : base + 24]
    return jnp.concatenate([values, extra], axis=0)


def pick(terms, targets, base):
    spots = iota((CAP, targets.shape[1]), 0) + base
    return dot_nt(terms, (spots == targets).astype(F32).astype(BF16))


def fold(value, count):
    return jnp.where(value >= count, value - count, value)


def step_kernel(
    dom_count, col_count, reach, links_ref, panel_hbm, blocks_hbm, rows_ref, parts_ref,
    basis_ref, residual_ref, gram_ref,
    panel_ref, blocks_ref, load_sems, panels, terms, send, arrived, local, terms_in, landing, pieces, others, parts, landed,
    mine, lines, total, whole, dom_sems, col_sems, part_sems, line_sems, whole_sems,
):
    dom, col = lax.axis_index("dom"), lax.axis_index("col")
    width = panel_ref.shape[0]
    coupled_count, node, entries = blocks_ref.shape
    elements = links_ref.shape[1]
    rs = entries // elements
    group = LANES // rs
    part = ROWS_DEV // col_count
    size = width * col_count

    def remote(source, target, sems, index, device):
        return pltpu.make_async_remote_copy(
            src_ref=source,
            dst_ref=target,
            send_sem=sems.at[0, index],
            recv_sem=sems.at[1, index],
            device_id=device,
            device_id_type=pl.DeviceIdType.MESH,
        )

    def dom_at(o):
        return fold(dom + o, dom_count), col

    def col_at(o):
        return dom, fold(col + o, col_count)

    def dom_copy(o):
        return remote(send.at[o - 1], arrived.at[o - 1], dom_sems, o - 1, dom_at(o))

    def col_copy(o):
        there = fold(col + o, col_count)
        return remote(pieces.at[there], others.at[col], col_sems, o - 1, col_at(o))

    def part_copy(o):
        there = fold(dom + o, dom_count)
        return remote(parts.at[there], landed.at[o - 1], part_sems, o - 1, dom_at(o))

    def line_copy(o):
        return remote(mine, lines.at[o - 1], line_sems, o - 1, col_at(o))

    def whole_copy(o):
        return remote(total, whole.at[dom], whole_sems, o - 1, dom_at(o))

    panel_load = pltpu.make_async_copy(panel_hbm, panel_ref, load_sems.at[0])
    blocks_load = pltpu.make_async_copy(blocks_hbm, blocks_ref, load_sems.at[1])
    panel_load.start()
    blocks_load.start()
    barrier = pltpu.get_barrier_semaphore()

    for count, device_at in ((dom_count, dom_at), (col_count, col_at)):

        @pl.loop(1, count)
        def _(o, device_at=device_at):
            pl.semaphore_signal(
                barrier, inc=1, device_id=device_at(o), device_id_type=pl.DeviceIdType.MESH
            )

    shift = ROWS_DEV.bit_length() - 1
    match_rows = max(16, dom_count)
    before = (iota((LANES, LANES), 0) < iota((LANES, LANES), 1)).astype(F32).astype(BF16)
    carry = jnp.zeros((match_rows, 1), F32)
    targets = []
    for start in range(0, entries, LANES):
        rows = rows_ref[:, start : start + LANES]
        offset = fold((rows >> shift) - dom + dom_count, dom_count)
        local_row = rows & (ROWS_DEV - 1)
        matches = (iota((match_rows, LANES), 0) == offset).astype(F32)
        ranks = jnp.sum(
            matches * (dot_nn(matches.astype(BF16), before) + carry), axis=0, keepdims=True
        ).astype(jnp.int32)
        carry = carry + jnp.sum(matches, axis=1, keepdims=True)
        targets.append(
            jnp.where(offset == 0, local_row, ROWS_DEV + (offset - 1) * CAP + ranks)
        )
    targets = jnp.concatenate(targets, axis=1)

    row_values = (rows_ref[...] & (ROWS_DEV - 1)).astype(F32)
    which = iota((8, entries), 0)
    extra = jnp.where(which == 0, parts_ref[...], jnp.where(which == 1, row_values, 0.0))
    terms[2 * width :, :] = split_extra(extra)

    panel_load.wait()

    @pl.loop(0, elements // 2, unroll=4)
    def _(pair):
        window = panel_ref[:, pl.ds(pl.multiple_of(pair * 2 * node, LANES), 2 * node)]
        panels[2 * pair] = window[:, :node]
        panels[2 * pair + 1] = window[:, node:]

    lane_element = iota((width, LANES), 1) // rs

    blocks_load.wait()

    @pl.loop(0, elements // group, unroll=4)
    def _(block):
        columns = pl.ds(pl.multiple_of(block * LANES, LANES), LANES)
        found = jnp.zeros((group * width, LANES), F32)
        for coupled in range(coupled_count):
            picked = jnp.concatenate(
                [panels[links_ref[coupled, block * group + q]] for q in range(group)], axis=0
            )
            found = found + dot_nn(picked, blocks_ref[coupled, :, columns])
        out = found[:width]
        for q in range(1, group):
            out = jnp.where(lane_element == q, found[q * width : (q + 1) * width], out)
        high, low = split_values(out)
        terms[:width, columns] = high
        terms[width : 2 * width, columns] = low

    pl.semaphore_wait(barrier, dom_count + col_count - 2)

    @pl.loop(1, reach + 1)
    def _(o):
        send[o - 1] = join(pick(terms[...], targets, ROWS_DEV + (o - 1) * CAP), width)
        dom_copy(o).start()

    @pl.loop(0, ROWS_DEV // CAP)
    def _(tile):
        base = tile * CAP
        local[:, pl.ds(pl.multiple_of(base, CAP), CAP)] = join(
            pick(terms[...], targets, base), width
        )

    for o in range(1, reach + 1):
        dom_copy(o).wait_recv()
        columns = slice((o - 1) * CAP, o * CAP)
        high, low = split_values(arrived[o - 1, :width, :])
        terms_in[:width, columns] = high
        terms_in[width : 2 * width, columns] = low
        extra = arrived[o - 1, width:, :]
        terms_in[2 * width :, columns] = split_extra(extra)
        landing[:, columns] = extra[1:2, :].astype(jnp.int32)
    targets = landing[...]

    def assemble(base):
        columns = pl.ds(pl.multiple_of(base, CAP), CAP)
        found = join(pick(terms_in[...], targets, base), width) + local[:, columns]
        basis_ref[:, columns] = found[:width]
        residual_ref[:, columns] = found[width : width + 1]
        return found

    if part == CAP:

        @pl.loop(1, col_count)
        def _(o):
            there = fold(col + o, col_count)
            pieces[there] = assemble(there * part)[:width]
            col_copy(o).start()

        found = assemble(col * part)
        others[col] = found[:width]
        own_residual = found[width : width + 1]
    else:
        for tile in range(ROWS_DEV // CAP):
            assemble(tile * CAP)
        own_residual = jnp.zeros((1, part), F32)
        for index in range(col_count):
            columns = slice(index * part, (index + 1) * part)
            pieces[index] = basis_ref[:, columns]
            own_residual = own_residual + jnp.where(index == col, residual_ref[:, columns], 0.0)
        for o in range(1, col_count):
            col_copy(o).start()
        others[col] = pieces[col]
    for o in range(1, col_count):
        col_copy(o).wait_recv()

    half = size // 2
    basis = others[...].reshape(size, part)
    top, bottom = basis[:half], basis[half:]
    first = dot_nt(top, top, HIGHEST)
    cross = dot_nt(top, bottom, HIGHEST)
    second = dot_nt(bottom, bottom, HIGHEST)
    gradient = dot_nt(jnp.broadcast_to(own_residual, (8, part)), basis, HIGHEST)[:1]
    row, column = iota((half, half), 0), iota((half, half), 1)
    diagonal = jnp.sum(jnp.where(row == column, second, 0.0), axis=0, keepdims=True)
    packed = jnp.concatenate([jnp.where(row <= column, first, second), cross], axis=0)
    rows = size // dom_count
    spare = [diagonal, gradient[:, :half], gradient[:, half:]]
    for index in range(dom_count):
        parts[index, :rows] = packed[index * rows : (index + 1) * rows]
        parts[index, rows:] = spare[index] if index < 3 else jnp.zeros((1, half), F32)

    def exchange(copy, count):
        @pl.loop(1, count)
        def _(o):
            copy(o).start()

    def finish(copy, count):
        @pl.loop(1, count)
        def _(o):
            copy(o).wait_recv()

    exchange(part_copy, dom_count)
    finish(part_copy, dom_count)
    mine[...] = jnp.sum(landed[...], axis=0) + parts[dom]
    exchange(line_copy, col_count)
    finish(line_copy, col_count)
    total[...] = jnp.sum(lines[...], axis=0) + mine[...]
    exchange(whole_copy, dom_count)
    whole[dom] = total[...]
    finish(whole_copy, dom_count)
    gram_ref[...] = whole[...]
    for o in range(1, reach + 1):
        dom_copy(o).wait_send()

    @pl.loop(1, col_count)
    def _(o):
        col_copy(o).wait_send()
        line_copy(o).wait_send()

    @pl.loop(1, dom_count)
    def _(o):
        part_copy(o).wait_send()
        whole_copy(o).wait_send()


def tree_sum(terms):
    while len(terms) > 1:
        odd = [terms[-1]] if len(terms) % 2 else []
        terms = [a + b for a, b in zip(terms[::2], terms[1::2])] + odd
    return terms[0]


def split_three(x):
    high = x.astype(BF16)
    rest = x - high.astype(F32)
    middle = rest.astype(BF16)
    return high, middle, (rest - middle.astype(F32)).astype(BF16)


def product(a, b):
    ah, am, al = split_three(a)
    bh, bm, bl = split_three(b)

    def pair(a1, b1, a2, b2):
        return dot_nn(
            jnp.concatenate([a1, a2], axis=1), jnp.concatenate([b1, b2], axis=0)
        )

    return pair(ah, bh, am, bh) + (pair(ah, bm, am, bm) + pair(ah, bl, al, bh))


def eliminate(matrix, side):
    size = matrix.shape[0]
    shape = (8, size)
    row, lane = iota(shape, 0), iota(shape, 1)
    tall = PIVOTS // 8
    wide = [matrix, side]
    groups = [[w[k : k + 8] for w in wide] for k in range(0, size, 8)]

    def column(x, k):
        return jnp.broadcast_to(x[:, k : k + 1], shape)

    def across(x, r):
        return jnp.broadcast_to(x[r : r + 1], shape)

    for start in range(0, size, PIVOTS):
        first = start // 8
        last = first + tall
        inside = (lane >= start) & (lane < start + PIVOTS)

        def kept(g):
            return [jnp.where(inside, 0.0, groups[g][0])] + groups[g][1:]

        panel = groups[first:last]
        columns = [[column(p[0], start + j) for j in range(PIVOTS)] for p in panel]
        work = [
            [jnp.where(inside, (lane - start - 8 * t == row).astype(F32), p[0])] + p[1:]
            for t, p in enumerate(panel)
        ]
        scales = [None] * tall
        for i in range(PIVOTS):
            own, r = divmod(i, 8)
            here = row == r
            scale = 1.0 / across(columns[own][i], r)
            factors = [columns[t][i] * scale for t in range(tall)]
            factors[own] = jnp.where(here, 0.0, factors[own])
            scales[own] = scale if r == 0 else jnp.where(here, scale, scales[own])
            for j in range(i + 1, PIVOTS):
                moved = across(columns[own][j], r)
                for t in range(tall):
                    columns[t][j] = columns[t][j] - factors[t] * moved
            for w in range(len(wide)):
                moved = across(work[own][w], r)
                for t in range(tall):
                    work[t][w] = work[t][w] - factors[t] * moved
        done = [[x * scales[t] for x in work[t]] for t in range(tall)]
        ahead = {}
        for g in range(last, min(last + tall, len(groups))):
            cols = [column(groups[g][0], start + k) for k in range(PIVOTS)]
            ahead[g] = [
                x - tree_sum([cols[k] * across(done[k // 8][w], k % 8) for k in range(PIVOTS)])
                for w, x in enumerate(kept(g))
            ]
        left = jnp.concatenate([jnp.where(inside, g[0], 0.0) for g in groups], axis=0)
        empty = [jnp.zeros(shape, F32)] * len(wide)
        right = jnp.concatenate(
            [
                jnp.concatenate(done[g - first] if first <= g < last else empty, axis=1)
                for g in range(len(groups))
            ],
            axis=0,
        )
        change = product(left, right)
        for g in range(len(groups)):
            if first <= g < last:
                groups[g] = done[g - first]
            elif g in ahead:
                groups[g] = ahead[g]
            else:
                rows = change[8 * g : 8 * g + 8]
                groups[g] = [
                    x - rows[:, size * w : size * (w + 1)] for w, x in enumerate(kept(g))
                ]
    return [jnp.concatenate([g[w] for g in groups], axis=0) for w in range(len(wide))]


def solve_kernel(
    col_ref, gram_ref, basis_ref, residual_ref, out_ref, basis_out_ref, residual_out_ref
):
    basis_out_ref[...] = basis_ref[...]
    residual_out_ref[...] = residual_ref[...]
    dom_count, height, half = gram_ref.shape
    size = 2 * half
    rows = height - 1
    row, column = iota((half, half), 0), iota((half, half), 1)

    def block(start):
        return jnp.concatenate(
            [gram_ref[start // rows + k, :rows] for k in range(half // rows)], axis=0
        )

    spare = [gram_ref[index, rows:] for index in range(3)]
    square, cross = block(0), block(half)
    turned = square.T
    first = jnp.where(row <= column, square, turned)
    second = jnp.where(row < column, turned, jnp.where(row == column, spare[0], square))
    first_inverse, carried = eliminate(first, cross)
    second = second - dot_tn(cross, carried, HIGHEST)
    top = jnp.broadcast_to(spare[1], (8, half))
    x_top = dot_nn(top, first_inverse, HIGHEST)[:1]
    low = spare[2] - dot_nn(top, carried, HIGHEST)[:1]
    low = jnp.broadcast_to(low, (half, half)).T
    second_inverse, back = eliminate(second, -carried.T)
    x_bottom = jnp.sum(low * second_inverse, axis=0, keepdims=True)
    x_top = x_top + jnp.sum(low * back, axis=0, keepdims=True)
    full = -jnp.concatenate([x_top, x_bottom], axis=1)
    width = out_ref.shape[1]
    out = jnp.zeros((1, width), F32)
    for index in range(size // width):
        out = jnp.where(col_ref[0] == index, full[:, index * width : (index + 1) * width], out)
    out_ref[...] = out


VMEM = pl.BlockSpec(memory_space=pltpu.VMEM)
SMEM = pl.BlockSpec(memory_space=pltpu.SMEM)
ANY = pl.BlockSpec(memory_space=pl.ANY)


def body(basis_panel, jacobian, neighbors, sample_rows, residual_parts):
    dom_count, col_count = lax.axis_size("dom"), lax.axis_size("col")
    col_index = lax.axis_index("col")
    width = basis_panel.shape[0]
    entries = sample_rows.shape[0]
    elements = neighbors.shape[0]
    node = jacobian.shape[1]
    size = width * col_count
    shape = jax.ShapeDtypeStruct
    reach = min(dom_count - 1, REACH_MOST)
    part = ROWS_DEV // col_count
    chunk = (size // dom_count + 1, size // 2)
    jacobian_basis, sampled_residual, whole = pl.pallas_call(
        functools.partial(step_kernel, dom_count, col_count, reach),
        out_shape=(
            shape((width, ROWS_DEV), F32), shape((1, ROWS_DEV), F32), shape((dom_count,) + chunk, F32)
        ),
        in_specs=[SMEM, ANY, ANY, VMEM, VMEM],
        out_specs=(VMEM, VMEM, VMEM),
        scratch_shapes=[
            pltpu.VMEM(basis_panel.shape, BF16),
            pltpu.VMEM(jacobian.shape, BF16),
            pltpu.SemaphoreType.DMA((2,)),
            pltpu.VMEM((elements, width, node), BF16),
            pltpu.VMEM((2 * width + 32, entries), BF16),
            pltpu.VMEM((reach, width + 8, CAP), F32),
            pltpu.VMEM((reach, width + 8, CAP), F32),
            pltpu.VMEM((width + 8, ROWS_DEV), F32),
            pltpu.VMEM((2 * width + 32, reach * CAP), BF16),
            pltpu.VMEM((1, reach * CAP), jnp.int32),
            pltpu.VMEM((col_count, width, part), F32),
            pltpu.VMEM((col_count, width, part), F32),
            pltpu.VMEM((dom_count,) + chunk, F32),
            pltpu.VMEM((dom_count - 1,) + chunk, F32),
            pltpu.VMEM(chunk, F32),
            pltpu.VMEM((col_count - 1,) + chunk, F32),
            pltpu.VMEM(chunk, F32),
            pltpu.VMEM((dom_count,) + chunk, F32),
            pltpu.SemaphoreType.DMA((2, reach)),
            pltpu.SemaphoreType.DMA((2, col_count - 1)),
            pltpu.SemaphoreType.DMA((2, dom_count - 1)),
            pltpu.SemaphoreType.DMA((2, col_count - 1)),
            pltpu.SemaphoreType.DMA((2, dom_count - 1)),
        ],
        compiler_params=pltpu.CompilerParams(collective_id=0, has_side_effects=True),
        name="step",
    )(
        neighbors.T,
        basis_panel,
        jacobian,
        sample_rows.reshape(1, entries),
        residual_parts.reshape(1, entries),
    )
    reduced_step, jacobian_basis, sampled_residual = pl.pallas_call(
        solve_kernel,
        out_shape=(
            shape((1, width), F32), shape((width, ROWS_DEV), F32), shape((1, ROWS_DEV), F32)
        ),
        in_specs=[SMEM, VMEM, VMEM, VMEM],
        out_specs=(VMEM, VMEM, VMEM),
        name="solve",
    )(
        col_index.astype(jnp.int32).reshape(1),
        whole,
        jacobian_basis,
        sampled_residual,
    )
    return (jacobian_basis, sampled_residual[0], reduced_step[0])


def solution(mesh):
    placed = (P("col", "dom"), P(None, None, "dom"), P("dom", None), P("dom"), P("dom"))
    return jax.shard_map(
        body,
        mesh=mesh,
        in_specs=placed,
        out_specs=(P("col", "dom"), P("dom"), P("col")),
        check_vma=False,
    )
```

```python
import functools

import jax
import jax.numpy as jnp
from jax import lax
from jax.experimental import pallas as pl
from jax.experimental.pallas import tpu as pltpu
from jax.sharding import PartitionSpec as P

ROWS_DEV = 1024
CAP = 256
REACH_MOST = 8
LANES = 128
PIVOTS = 16
HIGHEST = lax.Precision.HIGHEST
F32 = jnp.float32
BF16 = jnp.bfloat16


def iota(shape, dim):
    return lax.broadcasted_iota(jnp.int32, shape, dim)


def dot_nn(a, b, precision=None):
    return lax.dot_general(
        a, b, (((1,), (0,)), ((), ())), precision=precision, preferred_element_type=F32
    )


def dot_nt(a, b, precision=None):
    return lax.dot_general(
        a, b, (((1,), (1,)), ((), ())), precision=precision, preferred_element_type=F32
    )


def dot_tn(a, b, precision=None):
    return lax.dot_general(
        a, b, (((0,), (0,)), ((), ())), precision=precision, preferred_element_type=F32
    )


def split_values(x):
    high = x.astype(BF16)
    return high, (x - high.astype(F32)).astype(BF16)


def split_extra(x):
    high = x.astype(BF16).astype(F32)
    middle = (x - high).astype(BF16).astype(F32)
    low = x - high - middle
    return jnp.concatenate([high, middle, low, jnp.zeros_like(x)], axis=0).astype(BF16)


def join(found, width):
    values = found[:width] + found[width : 2 * width]
    base = 2 * width
    extra = found[base : base + 8] + found[base + 8 : base + 16] + found[base + 16 : base + 24]
    return jnp.concatenate([values, extra], axis=0)


def pick(terms, targets, base):
    count = targets.shape[1]
    near = jnp.clip(targets - base, -1, CAP).astype(F32)
    near = jnp.broadcast_to(near, (16, count)).astype(BF16)
    near = jnp.concatenate([near] * (CAP // 16), axis=0)
    spots = iota((CAP, LANES), 0).astype(F32).astype(BF16)
    spots = jnp.concatenate([spots] * (count // LANES), axis=1)
    return dot_nt(terms, jnp.where(spots == near, 1.0, 0.0).astype(BF16))


def fold(value, count):
    return jnp.where(value >= count, value - count, value)


def step_kernel(
    dom_count, col_count, reach, links_ref, panel_hbm, blocks_hbm, rows_ref, parts_ref,
    basis_ref, residual_ref, gram_ref,
    panel_ref, blocks_ref, load_sems, panels, terms, send, send_late, arrived, arrived_late, local, terms_in, terms_late, landing, pieces, others, parts, landed,
    mine, lines, total, whole, dom_sems, col_sems, part_sems, line_sems, whole_sems,
):
    dom, col = lax.axis_index("dom"), lax.axis_index("col")
    width = panel_ref.shape[0]
    coupled_count, node, entries = blocks_ref.shape
    elements = links_ref.shape[1]
    rs = entries // elements
    group = LANES // rs
    part = ROWS_DEV // col_count
    size = width * col_count
    half_width = width // 2

    def remote(source, target, sems, index, device):
        return pltpu.make_async_remote_copy(
            src_ref=source,
            dst_ref=target,
            send_sem=sems.at[0, index],
            recv_sem=sems.at[1, index],
            device_id=device,
            device_id_type=pl.DeviceIdType.MESH,
        )

    def dom_at(o):
        return fold(dom + o, dom_count), col

    def col_at(o):
        return dom, fold(col + o, col_count)

    def offset_at(turn):
        if reach != dom_count - 1 or dom_count & reach:
            return turn + 1
        flips = jnp.where(turn < reach - 1, reach - 1 - turn // 2 * 2 + turn % 2, 1)
        partner, bit = 0, 1
        while bit < dom_count:
            partner = partner + (dom // bit + flips // bit) % 2 * bit
            bit *= 2
        return (dom_count + partner - dom) % dom_count

    def dom_copy(half, o):
        source, target = ((send, arrived), (send_late, arrived_late))[half]
        return remote(source.at[o - 1], target.at[o - 1], dom_sems, half * reach + o - 1, dom_at(o))

    def col_copy(half, o):
        there = fold(col + o, col_count)
        return remote(
            pieces.at[half, there], others.at[half, col],
            col_sems, half * (col_count - 1) + o - 1, col_at(o),
        )

    def part_copy(o):
        there = fold(dom + o, dom_count)
        return remote(parts.at[there], landed.at[o - 1], part_sems, o - 1, dom_at(o))

    def line_copy(o):
        return remote(mine, lines.at[o - 1], line_sems, o - 1, col_at(o))

    def whole_copy(o):
        return remote(total, whole.at[dom], whole_sems, o - 1, dom_at(o))

    panel_load = pltpu.make_async_copy(panel_hbm, panel_ref, load_sems.at[0])
    blocks_load = pltpu.make_async_copy(blocks_hbm, blocks_ref, load_sems.at[1])
    panel_load.start()
    blocks_load.start()
    barrier = pltpu.get_barrier_semaphore()

    for count, device_at in ((dom_count, dom_at), (col_count, col_at)):

        @pl.loop(1, count)
        def _(o, device_at=device_at):
            pl.semaphore_signal(
                barrier, inc=1, device_id=device_at(o), device_id_type=pl.DeviceIdType.MESH
            )

    shift = ROWS_DEV.bit_length() - 1
    match_rows = max(16, dom_count)
    before = (iota((LANES, LANES), 0) < iota((LANES, LANES), 1)).astype(F32).astype(BF16)
    carry = jnp.zeros((match_rows, 1), F32)
    targets = []
    for start in range(0, entries, LANES):
        rows = rows_ref[:, start : start + LANES]
        offset = fold((rows >> shift) - dom + dom_count, dom_count)
        local_row = rows & (ROWS_DEV - 1)
        matches = (iota((match_rows, LANES), 0) == offset).astype(F32)
        ranks = jnp.sum(
            matches * (dot_nn(matches.astype(BF16), before) + carry), axis=0, keepdims=True
        ).astype(jnp.int32)
        carry = carry + jnp.sum(matches, axis=1, keepdims=True)
        targets.append(
            jnp.where(offset == 0, local_row, ROWS_DEV + (offset - 1) * CAP + ranks)
        )
    targets = jnp.concatenate(targets, axis=1)

    row_values = (rows_ref[...] & (ROWS_DEV - 1)).astype(F32)
    which = iota((8, entries), 0)
    extra = jnp.where(which == 0, parts_ref[...], jnp.where(which == 1, row_values, 0.0))
    terms[2 * width :, :] = split_extra(extra)

    panel_load.wait()

    @pl.loop(0, elements // 2, unroll=4)
    def _(pair):
        window = panel_ref[:, pl.ds(pl.multiple_of(pair * 2 * node, LANES), 2 * node)]
        panels[2 * pair] = window[:, :node]
        panels[2 * pair + 1] = window[:, node:]

    lane_element = iota((width, LANES), 1) // rs

    blocks_load.wait()

    @pl.loop(0, elements // group, unroll=4)
    def _(block):
        columns = pl.ds(pl.multiple_of(block * LANES, LANES), LANES)
        found = jnp.zeros((group * width, LANES), F32)
        for coupled in range(coupled_count):
            picked = jnp.concatenate(
                [panels[links_ref[coupled, block * group + q]] for q in range(group)], axis=0
            )
            found = found + dot_nn(picked, blocks_ref[coupled, :, columns])
        out = found[:width]
        for q in range(1, group):
            out = jnp.where(lane_element == q, found[q * width : (q + 1) * width], out)
        high, low = split_values(out)
        terms[:width, columns] = high
        terms[width : 2 * width, columns] = low

    pl.semaphore_wait(barrier, dom_count + col_count - 2)

    @pl.loop(0, reach)
    def _(turn):
        o = offset_at(turn)
        found = join(pick(terms[...], targets, ROWS_DEV + (o - 1) * CAP), width)
        send[o - 1, :half_width] = found[:half_width]
        send[o - 1, half_width:] = found[width:]
        send_late[o - 1] = found[half_width:width]
        dom_copy(0, o).start()

    @pl.loop(0, reach)
    def _(turn):
        dom_copy(1, offset_at(turn)).start()

    @pl.loop(0, ROWS_DEV // CAP)
    def _(tile):
        base = tile * CAP
        local[:, pl.ds(pl.multiple_of(base, CAP), CAP)] = join(
            pick(terms[...], targets, base), width
        )

    def assemble(half, base):
        columns = pl.ds(pl.multiple_of(base, CAP), CAP)
        found = pick((terms_in, terms_late)[half][...], landing[...], base)
        start = half * half_width
        values = found[:half_width] + found[half_width : 2 * half_width]
        values = values + local[start : start + half_width, columns]
        basis_ref[start : start + half_width, columns] = values
        if half == 0:
            extra = found[2 * half_width :]
            extra = extra[:8] + extra[8:16] + extra[16:24] + local[width:, columns]
            residual_ref[:, columns] = extra[:1]
        return values

    def pass_on(half):
        if part == CAP:

            @pl.loop(1, col_count)
            def _(o):
                there = fold(col + o, col_count)
                pieces[half, there] = assemble(half, there * part)
                col_copy(half, o).start()

            others[half, col] = assemble(half, col * part)
            return
        for tile in range(ROWS_DEV // CAP):
            assemble(half, tile * CAP)
        rows = slice(half * half_width, (half + 1) * half_width)
        for index in range(col_count):
            pieces[half, index] = basis_ref[rows, index * part : (index + 1) * part]

        @pl.loop(1, col_count)
        def _(o):
            col_copy(half, o).start()

        others[half, col] = pieces[half, col]

    for o in range(1, reach + 1):
        dom_copy(0, o).wait_recv()
        columns = slice((o - 1) * CAP, o * CAP)
        block = arrived[o - 1]
        extra = block[half_width:]
        high, low = split_values(block[:half_width])
        terms_in[:, columns] = jnp.concatenate([high, low, split_extra(extra)], axis=0)
        landing[:, columns] = extra[1:2].astype(jnp.int32)

    pass_on(0)
    own_residual = jnp.zeros((1, part), F32)
    for index in range(col_count):
        piece = residual_ref[:, index * part : (index + 1) * part]
        own_residual = own_residual + jnp.where(index == col, piece, 0.0)

    for o in range(1, reach + 1):
        dom_copy(1, o).wait_recv()
        high, low = split_values(arrived_late[o - 1])
        terms_late[:, (o - 1) * CAP : o * CAP] = jnp.concatenate([high, low], axis=0)

    pass_on(1)
    for o in range(1, col_count):
        col_copy(0, o).wait_recv()
    half = size // 2
    top = others[0].reshape(half, part)
    first = dot_nt(top, top, HIGHEST)
    for o in range(1, col_count):
        col_copy(1, o).wait_recv()
    bottom = others[1].reshape(half, part)
    basis = jnp.concatenate([top, bottom], axis=0)
    cross = dot_nt(top, bottom, HIGHEST)
    second = dot_nt(bottom, bottom, HIGHEST)
    gradient = dot_nt(jnp.broadcast_to(own_residual, (8, part)), basis, HIGHEST)[:1]
    row, column = iota((half, half), 0), iota((half, half), 1)
    diagonal = jnp.sum(jnp.where(row == column, second, 0.0), axis=0, keepdims=True)
    packed = jnp.concatenate([jnp.where(row <= column, first, second), cross], axis=0)
    rows = size // dom_count
    spare = [diagonal, gradient[:, :half], gradient[:, half:]]
    for index in range(dom_count):
        parts[index, :rows] = packed[index * rows : (index + 1) * rows]
        parts[index, rows:] = spare[index] if index < 3 else jnp.zeros((1, half), F32)

    def exchange(copy, count):
        @pl.loop(1, count)
        def _(o):
            copy(o).start()

    def finish(copy, count):
        @pl.loop(1, count)
        def _(o):
            copy(o).wait_recv()

    exchange(part_copy, dom_count)
    finish(part_copy, dom_count)
    mine[...] = jnp.sum(landed[...], axis=0) + parts[dom]
    exchange(line_copy, col_count)
    finish(line_copy, col_count)
    total[...] = jnp.sum(lines[...], axis=0) + mine[...]
    exchange(whole_copy, dom_count)
    whole[dom] = total[...]
    finish(whole_copy, dom_count)
    gram_ref[...] = whole[...]
    @pl.loop(1, reach + 1)
    def _(o):
        dom_copy(0, o).wait_send()
        dom_copy(1, o).wait_send()

    @pl.loop(1, col_count)
    def _(o):
        col_copy(0, o).wait_send()
        col_copy(1, o).wait_send()
        line_copy(o).wait_send()

    @pl.loop(1, dom_count)
    def _(o):
        part_copy(o).wait_send()
        whole_copy(o).wait_send()


def tree_sum(terms):
    while len(terms) > 1:
        odd = [terms[-1]] if len(terms) % 2 else []
        terms = [a + b for a, b in zip(terms[::2], terms[1::2])] + odd
    return terms[0]


def split_three(x):
    high = x.astype(BF16)
    rest = x - high.astype(F32)
    middle = rest.astype(BF16)
    return high, middle, (rest - middle.astype(F32)).astype(BF16)


def product(a, b):
    ah, am, al = split_three(a)
    bh, bm, bl = split_three(b)

    def pair(a1, b1, a2, b2):
        return dot_nn(
            jnp.concatenate([a1, a2], axis=1), jnp.concatenate([b1, b2], axis=0)
        )

    return pair(ah, bh, am, bh) + (pair(ah, bm, am, bm) + pair(ah, bl, al, bh))


def eliminate(matrix, side):
    size = matrix.shape[0]
    shape = (8, size)
    row, lane = iota(shape, 0), iota(shape, 1)
    tall = PIVOTS // 8
    wide = [matrix, side]
    groups = [[w[k : k + 8] for w in wide] for k in range(0, size, 8)]

    def column(x, k):
        return jnp.broadcast_to(x[:, k : k + 1], shape)

    def across(x, r):
        return jnp.broadcast_to(x[r : r + 1], shape)

    for start in range(0, size, PIVOTS):
        first = start // 8
        last = first + tall
        inside = (lane >= start) & (lane < start + PIVOTS)

        def kept(g):
            return [jnp.where(inside, 0.0, groups[g][0])] + groups[g][1:]

        panel = groups[first:last]
        columns = [[column(p[0], start + j) for j in range(PIVOTS)] for p in panel]
        work = [
            [jnp.where(inside, (lane - start - 8 * t == row).astype(F32), p[0])] + p[1:]
            for t, p in enumerate(panel)
        ]
        scales = [None] * tall
        for i in range(PIVOTS):
            own, r = divmod(i, 8)
            here = row == r
            scale = 1.0 / across(columns[own][i], r)
            factors = [columns[t][i] * scale for t in range(tall)]
            factors[own] = jnp.where(here, 0.0, factors[own])
            scales[own] = scale if r == 0 else jnp.where(here, scale, scales[own])
            for j in range(i + 1, PIVOTS):
                moved = across(columns[own][j], r)
                for t in range(tall):
                    columns[t][j] = columns[t][j] - factors[t] * moved
            for w in range(len(wide)):
                moved = across(work[own][w], r)
                for t in range(tall):
                    work[t][w] = work[t][w] - factors[t] * moved
        done = [[x * scales[t] for x in work[t]] for t in range(tall)]
        ahead = {}
        for g in range(last, min(last + tall, len(groups))):
            cols = [column(groups[g][0], start + k) for k in range(PIVOTS)]
            ahead[g] = [
                x - tree_sum([cols[k] * across(done[k // 8][w], k % 8) for k in range(PIVOTS)])
                for w, x in enumerate(kept(g))
            ]
        left = jnp.concatenate([jnp.where(inside, g[0], 0.0) for g in groups], axis=0)
        empty = [jnp.zeros(shape, F32)] * len(wide)
        right = jnp.concatenate(
            [
                jnp.concatenate(done[g - first] if first <= g < last else empty, axis=1)
                for g in range(len(groups))
            ],
            axis=0,
        )
        change = product(left, right)
        for g in range(len(groups)):
            if first <= g < last:
                groups[g] = done[g - first]
            elif g in ahead:
                groups[g] = ahead[g]
            else:
                rows = change[8 * g : 8 * g + 8]
                groups[g] = [
                    x - rows[:, size * w : size * (w + 1)] for w, x in enumerate(kept(g))
                ]
    return [jnp.concatenate([g[w] for g in groups], axis=0) for w in range(len(wide))]


def solve_kernel(
    col_ref, gram_ref, basis_ref, residual_ref, out_ref, basis_out_ref, residual_out_ref
):
    basis_out_ref[...] = basis_ref[...]
    residual_out_ref[...] = residual_ref[...]
    dom_count, height, half = gram_ref.shape
    size = 2 * half
    rows = height - 1
    row, column = iota((half, half), 0), iota((half, half), 1)

    def block(start):
        return jnp.concatenate(
            [gram_ref[start // rows + k, :rows] for k in range(half // rows)], axis=0
        )

    spare = [gram_ref[index, rows:] for index in range(3)]
    square, cross = block(0), block(half)
    turned = square.T
    first = jnp.where(row <= column, square, turned)
    second = jnp.where(row < column, turned, jnp.where(row == column, spare[0], square))
    first_inverse, carried = eliminate(first, cross)
    second = second - dot_tn(cross, carried, HIGHEST)
    top = jnp.broadcast_to(spare[1], (8, half))
    x_top = dot_nn(top, first_inverse, HIGHEST)[:1]
    low = spare[2] - dot_nn(top, carried, HIGHEST)[:1]
    low = jnp.broadcast_to(low, (half, half)).T
    second_inverse, back = eliminate(second, -carried.T)
    x_bottom = jnp.sum(low * second_inverse, axis=0, keepdims=True)
    x_top = x_top + jnp.sum(low * back, axis=0, keepdims=True)
    width = out_ref.shape[1]
    out = jnp.zeros((1, width), F32)
    for index in range(size // width):
        mine = slice(index * width // 2, (index + 1) * width // 2)
        own = -jnp.concatenate([x_top[:, mine], x_bottom[:, mine]], axis=1)
        out = jnp.where(col_ref[0] == index, own, out)
    out_ref[...] = out


VMEM = pl.BlockSpec(memory_space=pltpu.VMEM)
SMEM = pl.BlockSpec(memory_space=pltpu.SMEM)
ANY = pl.BlockSpec(memory_space=pl.ANY)


def body(basis_panel, jacobian, neighbors, sample_rows, residual_parts):
    dom_count, col_count = lax.axis_size("dom"), lax.axis_size("col")
    col_index = lax.axis_index("col")
    width = basis_panel.shape[0]
    entries = sample_rows.shape[0]
    elements = neighbors.shape[0]
    node = jacobian.shape[1]
    size = width * col_count
    shape = jax.ShapeDtypeStruct
    reach = min(dom_count - 1, REACH_MOST)
    part = ROWS_DEV // col_count
    chunk = (size // dom_count + 1, size // 2)
    jacobian_basis, sampled_residual, whole = pl.pallas_call(
        functools.partial(step_kernel, dom_count, col_count, reach),
        out_shape=(
            shape((width, ROWS_DEV), F32), shape((1, ROWS_DEV), F32), shape((dom_count,) + chunk, F32)
        ),
        in_specs=[SMEM, ANY, ANY, VMEM, VMEM],
        out_specs=(VMEM, VMEM, VMEM),
        scratch_shapes=[
            pltpu.VMEM(basis_panel.shape, BF16),
            pltpu.VMEM(jacobian.shape, BF16),
            pltpu.SemaphoreType.DMA((2,)),
            pltpu.VMEM((elements, width, node), BF16),
            pltpu.VMEM((2 * width + 32, entries), BF16),
            pltpu.VMEM((reach, width // 2 + 8, CAP), F32),
            pltpu.VMEM((reach, width // 2, CAP), F32),
            pltpu.VMEM((reach, width // 2 + 8, CAP), F32),
            pltpu.VMEM((reach, width // 2, CAP), F32),
            pltpu.VMEM((width + 8, ROWS_DEV), F32),
            pltpu.VMEM((width + 32, reach * CAP), BF16),
            pltpu.VMEM((width, reach * CAP), BF16),
            pltpu.VMEM((1, reach * CAP), jnp.int32),
            pltpu.VMEM((2, col_count, width // 2, part), F32),
            pltpu.VMEM((2, col_count, width // 2, part), F32),
            pltpu.VMEM((dom_count,) + chunk, F32),
            pltpu.VMEM((dom_count - 1,) + chunk, F32),
            pltpu.VMEM(chunk, F32),
            pltpu.VMEM((col_count - 1,) + chunk, F32),
            pltpu.VMEM(chunk, F32),
            pltpu.VMEM((dom_count,) + chunk, F32),
            pltpu.SemaphoreType.DMA((2, 2 * reach)),
            pltpu.SemaphoreType.DMA((2, 2 * (col_count - 1))),
            pltpu.SemaphoreType.DMA((2, dom_count - 1)),
            pltpu.SemaphoreType.DMA((2, col_count - 1)),
            pltpu.SemaphoreType.DMA((2, dom_count - 1)),
        ],
        compiler_params=pltpu.CompilerParams(collective_id=0, has_side_effects=True),
        name="step",
    )(
        neighbors.T,
        basis_panel,
        jacobian,
        sample_rows.reshape(1, entries),
        residual_parts.reshape(1, entries),
    )
    reduced_step, jacobian_basis, sampled_residual = pl.pallas_call(
        solve_kernel,
        out_shape=(
            shape((1, width), F32), shape((width, ROWS_DEV), F32), shape((1, ROWS_DEV), F32)
        ),
        in_specs=[SMEM, VMEM, VMEM, VMEM],
        out_specs=(VMEM, VMEM, VMEM),
        name="solve",
    )(
        col_index.astype(jnp.int32).reshape(1),
        whole,
        jacobian_basis,
        sampled_residual,
    )
    return (jacobian_basis, sampled_residual[0], reduced_step[0])


def solution(mesh):
    placed = (P("col", "dom"), P(None, None, "dom"), P("dom", None), P("dom"), P("dom"))
    return jax.shard_map(
        body,
        mesh=mesh,
        in_specs=placed,
        out_specs=(P("col", "dom"), P("dom"), P("col")),
        check_vma=False,
    )
```

```python
import functools

import jax
import jax.numpy as jnp
from jax import lax
from jax.experimental import pallas as pl
from jax.experimental.pallas import tpu as pltpu
from jax.sharding import PartitionSpec as P

ROWS_DEV = 1024
CAP = 256
REACH_MOST = 8
LANES = 128
PIVOTS = 16
VMEM_BYTES = 62 * 2**20
HIGHEST = lax.Precision.HIGHEST
F32 = jnp.float32
BF16 = jnp.bfloat16


def iota(shape, dim):
    return lax.broadcasted_iota(jnp.int32, shape, dim)


def dot_nn(a, b, precision=None):
    return lax.dot_general(
        a, b, (((1,), (0,)), ((), ())), precision=precision, preferred_element_type=F32
    )


def dot_nt(a, b, precision=None):
    return lax.dot_general(
        a, b, (((1,), (1,)), ((), ())), precision=precision, preferred_element_type=F32
    )


def dot_tn(a, b, precision=None):
    return lax.dot_general(
        a, b, (((0,), (0,)), ((), ())), precision=precision, preferred_element_type=F32
    )


def split_values(x):
    high = x.astype(BF16)
    return high, (x - high.astype(F32)).astype(BF16)


def split_extra(x):
    high = x.astype(BF16).astype(F32)
    middle = (x - high).astype(BF16).astype(F32)
    low = x - high - middle
    return jnp.concatenate([high, middle, low, jnp.zeros_like(x)], axis=0).astype(BF16)


def join(found, width):
    values = found[:width] + found[width : 2 * width]
    base = 2 * width
    extra = found[base : base + 8] + found[base + 8 : base + 16] + found[base + 16 : base + 24]
    return jnp.concatenate([values, extra], axis=0)


def spread_places(places, height):
    turned = jnp.concatenate(
        [
            jnp.broadcast_to(places[:, k : k + LANES], (LANES, LANES)).T
            for k in range(0, height, LANES)
        ],
        axis=0,
    )
    tile = turned >> (CAP.bit_length() - 1)
    return tile.astype(F32).astype(BF16), (turned & (CAP - 1)).astype(F32).astype(BF16)


def pick(terms, tiles, spots, tile):
    wanted = jnp.asarray(tile, jnp.int32).astype(F32)
    near = jnp.where(tiles == jnp.full(tiles.shape, wanted, F32).astype(BF16), spots, -1.0)
    lanes = [
        (iota(tiles.shape, 1) + start).astype(F32).astype(BF16) for start in range(0, CAP, LANES)
    ]
    chosen = jnp.concatenate([jnp.where(near == lane, 1.0, 0.0) for lane in lanes], axis=1)
    return dot_nn(terms, chosen.astype(BF16))


def pick_turned(terms, targets, base):
    count = targets.shape[1]
    near = jnp.clip(targets - base, -1, CAP).astype(F32)
    near = jnp.broadcast_to(near, (16, count)).astype(BF16)
    near = jnp.concatenate([near] * (CAP // 16), axis=0)
    spots = iota((CAP, LANES), 0).astype(F32).astype(BF16)
    spots = jnp.concatenate([spots] * (count // LANES), axis=1)
    return dot_nt(terms, jnp.where(spots == near, 1.0, 0.0).astype(BF16))


def fold(value, count):
    return jnp.where(value >= count, value - count, value)


def step_kernel(
    dom_count, col_count, reach, links_hbm, panel_hbm, blocks_hbm, rows_hbm, parts_hbm,
    basis_ref, residual_ref, gram_ref,
    links_ref, rows_ref, parts_ref, panel_ref, blocks_ref, load_sems, panels, terms, send, send_late, arrived, arrived_late, local, tiles_held, spots_held, terms_in, terms_late, landing, pieces, others, parts, landed,
    mine, lines, total, whole, dom_sems, col_sems, part_sems, line_sems, whole_sems,
):
    dom, col = lax.axis_index("dom"), lax.axis_index("col")
    width = panel_ref.shape[0]
    coupled_count, node, entries = blocks_ref.shape
    elements = links_ref.shape[1]
    rs = entries // elements
    group = LANES // rs
    part = ROWS_DEV // col_count
    size = width * col_count
    half_width = width // 2

    def remote(source, target, sems, index, device):
        return pltpu.make_async_remote_copy(
            src_ref=source,
            dst_ref=target,
            send_sem=sems.at[0, index],
            recv_sem=sems.at[1, index],
            device_id=device,
            device_id_type=pl.DeviceIdType.MESH,
        )

    def dom_at(o):
        return fold(dom + o, dom_count), col

    def col_at(o):
        return dom, fold(col + o, col_count)

    def offset_at(turn):
        if reach != dom_count - 1 or dom_count & reach:
            return turn + 1
        flips = jnp.where(turn < reach - 1, reach - 1 - turn // 2 * 2 + turn % 2, 1)
        partner, bit = 0, 1
        while bit < dom_count:
            partner = partner + (dom // bit + flips // bit) % 2 * bit
            bit *= 2
        return (dom_count + partner - dom) % dom_count

    def dom_copy(half, o):
        source, target = ((send, arrived), (send_late, arrived_late))[half]
        return remote(source.at[o - 1], target.at[o - 1], dom_sems, half * reach + o - 1, dom_at(o))

    def col_copy(half, o):
        there = fold(col + o, col_count)
        return remote(
            pieces.at[half, there], others.at[half, col],
            col_sems, half * (col_count - 1) + o - 1, col_at(o),
        )

    def part_copy(o):
        there = fold(dom + o, dom_count)
        return remote(parts.at[there], landed.at[o - 1], part_sems, o - 1, dom_at(o))

    def line_copy(o):
        return remote(mine, lines.at[o - 1], line_sems, o - 1, col_at(o))

    def whole_copy(o):
        return remote(total, whole.at[dom], whole_sems, o - 1, dom_at(o))

    panel_load = pltpu.make_async_copy(panel_hbm, panel_ref, load_sems.at[0])
    blocks_load = pltpu.make_async_copy(blocks_hbm, blocks_ref, load_sems.at[1])
    small_loads = [
        pltpu.make_async_copy(rows_hbm, rows_ref, load_sems.at[2]),
        pltpu.make_async_copy(parts_hbm, parts_ref, load_sems.at[3]),
        pltpu.make_async_copy(links_hbm, links_ref, load_sems.at[4]),
    ]
    for load in small_loads:
        load.start()
    panel_load.start()
    blocks_load.start()
    barrier = pltpu.get_barrier_semaphore()

    for count, device_at in ((dom_count, dom_at), (col_count, col_at)):

        @pl.loop(1, count)
        def _(o, device_at=device_at):
            pl.semaphore_signal(
                barrier, inc=1, device_id=device_at(o), device_id_type=pl.DeviceIdType.MESH
            )

    for load in small_loads:
        load.wait()
    shift = ROWS_DEV.bit_length() - 1
    match_rows = max(16, dom_count)
    before = (iota((LANES, LANES), 0) < iota((LANES, LANES), 1)).astype(F32).astype(BF16)
    carry = jnp.zeros((match_rows, 1), F32)
    targets = []
    for start in range(0, entries, LANES):
        rows = rows_ref[:, start : start + LANES]
        offset = fold((rows >> shift) - dom + dom_count, dom_count)
        local_row = rows & (ROWS_DEV - 1)
        matches = (iota((match_rows, LANES), 0) == offset).astype(F32)
        ranks = jnp.sum(
            matches * (dot_nn(matches.astype(BF16), before) + carry), axis=0, keepdims=True
        ).astype(jnp.int32)
        carry = carry + jnp.sum(matches, axis=1, keepdims=True)
        targets.append(
            jnp.where(offset == 0, local_row, ROWS_DEV + (offset - 1) * CAP + ranks)
        )
    targets = jnp.concatenate(targets, axis=1)
    tiles_held[...], spots_held[...] = spread_places(targets, entries)

    row_values = (rows_ref[...] & (ROWS_DEV - 1)).astype(F32)
    which = iota((8, entries), 0)
    extra = jnp.where(which == 0, parts_ref[...], jnp.where(which == 1, row_values, 0.0))
    terms[2 * width :, :] = split_extra(extra)

    deep = panels.shape[2]
    no_columns = jnp.zeros((width, deep - node), BF16)
    no_rows = jnp.zeros((deep - node, LANES), BF16)
    panel_load.wait()

    @pl.loop(0, elements // 2, unroll=4)
    def _(pair):
        window = panel_ref[:, pl.ds(pl.multiple_of(pair * 2 * node, LANES), 2 * node)]
        for which in range(2):
            held = window[:, which * node : (which + 1) * node]
            panels[2 * pair + which] = jnp.concatenate([held, no_columns], axis=1)

    lane_element = iota((width, LANES), 1) // rs

    blocks_load.wait()

    @pl.loop(0, elements // group, unroll=16)
    def _(block):
        columns = pl.ds(pl.multiple_of(block * LANES, LANES), LANES)
        picked = jnp.concatenate(
            [
                jnp.concatenate(
                    [panels[links_ref[coupled, block * group + q]] for q in range(group)], axis=0
                )
                for coupled in range(coupled_count)
            ],
            axis=1,
        )
        against = []
        for coupled in range(coupled_count):
            against += [blocks_ref[coupled, :, columns], no_rows]
        found = dot_nn(picked, jnp.concatenate(against, axis=0))
        out = found[:width]
        for q in range(1, group):
            out = jnp.where(lane_element == q, found[q * width : (q + 1) * width], out)
        high, low = split_values(out)
        terms[:width, columns] = high
        terms[width : 2 * width, columns] = low

    pl.semaphore_wait(barrier, dom_count + col_count - 2)

    @pl.loop(0, reach)
    def _(turn):
        o = offset_at(turn)
        found = join(pick(terms[...], tiles_held[...], spots_held[...], ROWS_DEV // CAP + o - 1), width)
        send[o - 1, :half_width] = found[:half_width]
        send[o - 1, half_width:] = found[width:]
        send_late[o - 1] = found[half_width:width]
        dom_copy(0, o).start()

    @pl.loop(0, reach)
    def _(turn):
        dom_copy(1, offset_at(turn)).start()

    @pl.loop(0, ROWS_DEV // CAP)
    def _(tile):
        base = tile * CAP
        local[:, pl.ds(pl.multiple_of(base, CAP), CAP)] = join(
            pick(terms[...], tiles_held[...], spots_held[...], tile), width
        )

    def assemble(half, base):
        columns = pl.ds(pl.multiple_of(base, CAP), CAP)
        found = pick_turned((terms_in, terms_late)[half][...], landing[...], base)
        start = half * half_width
        values = found[:half_width] + found[half_width : 2 * half_width]
        values = values + local[start : start + half_width, columns]
        basis_ref[start : start + half_width, columns] = values
        if half == 0:
            extra = found[2 * half_width :]
            extra = extra[:8] + extra[8:16] + extra[16:24] + local[width:, columns]
            residual_ref[:, columns] = extra[:1]
        return values

    def pass_on(half):
        if part == CAP:

            @pl.loop(1, col_count)
            def _(o):
                there = fold(col + o, col_count)
                pieces[half, there] = assemble(half, there * part)
                col_copy(half, o).start()

            others[half, col] = assemble(half, col * part)
            return
        for tile in range(ROWS_DEV // CAP):
            assemble(half, tile * CAP)
        rows = slice(half * half_width, (half + 1) * half_width)
        for index in range(col_count):
            pieces[half, index] = basis_ref[rows, index * part : (index + 1) * part]

        @pl.loop(1, col_count)
        def _(o):
            col_copy(half, o).start()

        others[half, col] = pieces[half, col]

    for o in range(1, reach + 1):
        dom_copy(0, o).wait_recv()
        columns = slice((o - 1) * CAP, o * CAP)
        block = arrived[o - 1]
        extra = block[half_width:]
        high, low = split_values(block[:half_width])
        terms_in[:, columns] = jnp.concatenate([high, low, split_extra(extra)], axis=0)
        landing[:, columns] = extra[1:2].astype(jnp.int32)

    pass_on(0)
    own_residual = jnp.zeros((1, part), F32)
    for index in range(col_count):
        piece = residual_ref[:, index * part : (index + 1) * part]
        own_residual = own_residual + jnp.where(index == col, piece, 0.0)

    for o in range(1, reach + 1):
        dom_copy(1, o).wait_recv()
        high, low = split_values(arrived_late[o - 1])
        terms_late[:, (o - 1) * CAP : o * CAP] = jnp.concatenate([high, low], axis=0)

    pass_on(1)
    for o in range(1, col_count):
        col_copy(0, o).wait_recv()
    half = size // 2
    top = others[0].reshape(half, part)
    first = dot_nt(top, top, HIGHEST)
    for o in range(1, col_count):
        col_copy(1, o).wait_recv()
    bottom = others[1].reshape(half, part)
    basis = jnp.concatenate([top, bottom], axis=0)
    cross = dot_nt(top, bottom, HIGHEST)
    second = dot_nt(bottom, bottom, HIGHEST)
    gradient = dot_nt(jnp.broadcast_to(own_residual, (8, part)), basis, HIGHEST)[:1]
    row, column = iota((half, half), 0), iota((half, half), 1)
    diagonal = jnp.sum(jnp.where(row == column, second, 0.0), axis=0, keepdims=True)
    packed = jnp.concatenate([jnp.where(row <= column, first, second), cross], axis=0)
    rows = size // dom_count
    spare = [diagonal, gradient[:, :half], gradient[:, half:]]
    for index in range(dom_count):
        parts[index, :rows] = packed[index * rows : (index + 1) * rows]
        parts[index, rows:] = spare[index] if index < 3 else jnp.zeros((1, half), F32)

    def exchange(copy, count):
        @pl.loop(1, count)
        def _(o):
            copy(o).start()

    def finish(copy, count):
        @pl.loop(1, count)
        def _(o):
            copy(o).wait_recv()

    exchange(part_copy, dom_count)
    finish(part_copy, dom_count)
    mine[...] = jnp.sum(landed[...], axis=0) + parts[dom]
    exchange(line_copy, col_count)
    finish(line_copy, col_count)
    total[...] = jnp.sum(lines[...], axis=0) + mine[...]
    exchange(whole_copy, dom_count)
    whole[dom] = total[...]
    finish(whole_copy, dom_count)
    gram_ref[...] = whole[...]
    @pl.loop(1, reach + 1)
    def _(o):
        dom_copy(0, o).wait_send()
        dom_copy(1, o).wait_send()

    @pl.loop(1, col_count)
    def _(o):
        col_copy(0, o).wait_send()
        col_copy(1, o).wait_send()
        line_copy(o).wait_send()

    @pl.loop(1, dom_count)
    def _(o):
        part_copy(o).wait_send()
        whole_copy(o).wait_send()


def tree_sum(terms):
    while len(terms) > 1:
        odd = [terms[-1]] if len(terms) % 2 else []
        terms = [a + b for a, b in zip(terms[::2], terms[1::2])] + odd
    return terms[0]


def split_three(x):
    high = x.astype(BF16)
    rest = x - high.astype(F32)
    middle = rest.astype(BF16)
    return high, middle, (rest - middle.astype(F32)).astype(BF16)


def product(a, b):
    ah, am, al = split_three(a)
    bh, bm, bl = split_three(b)

    def pair(a1, b1, a2, b2):
        return dot_nn(
            jnp.concatenate([a1, a2], axis=1), jnp.concatenate([b1, b2], axis=0)
        )

    return pair(ah, bh, am, bh) + (pair(ah, bm, am, bm) + pair(ah, bl, al, bh))


def eliminate(matrix, side):
    size = matrix.shape[0]
    shape = (8, size)
    row, lane = iota(shape, 0), iota(shape, 1)
    tall = PIVOTS // 8
    wide = [matrix, side]
    groups = [[w[k : k + 8] for w in wide] for k in range(0, size, 8)]

    def column(x, k):
        return jnp.broadcast_to(x[:, k : k + 1], shape)

    def across(x, r):
        return jnp.broadcast_to(x[r : r + 1], shape)

    for start in range(0, size, PIVOTS):
        first = start // 8
        last = first + tall
        inside = (lane >= start) & (lane < start + PIVOTS)

        def kept(g):
            return [jnp.where(inside, 0.0, groups[g][0])] + groups[g][1:]

        panel = groups[first:last]
        columns = [[column(p[0], start + j) for j in range(PIVOTS)] for p in panel]
        work = [
            [jnp.where(inside, (lane - start - 8 * t == row).astype(F32), p[0])] + p[1:]
            for t, p in enumerate(panel)
        ]
        scales = [None] * tall
        for i in range(PIVOTS):
            own, r = divmod(i, 8)
            here = row == r
            scale = 1.0 / across(columns[own][i], r)
            factors = [columns[t][i] * scale for t in range(tall)]
            factors[own] = jnp.where(here, 0.0, factors[own])
            scales[own] = scale if r == 0 else jnp.where(here, scale, scales[own])
            for j in range(i + 1, PIVOTS):
                moved = across(columns[own][j], r)
                for t in range(tall):
                    columns[t][j] = columns[t][j] - factors[t] * moved
            for w in range(len(wide)):
                moved = across(work[own][w], r)
                for t in range(tall):
                    work[t][w] = work[t][w] - factors[t] * moved
        done = [[x * scales[t] for x in work[t]] for t in range(tall)]
        ahead = {}
        for g in range(last, min(last + tall, len(groups))):
            cols = [column(groups[g][0], start + k) for k in range(PIVOTS)]
            ahead[g] = [
                x - tree_sum([cols[k] * across(done[k // 8][w], k % 8) for k in range(PIVOTS)])
                for w, x in enumerate(kept(g))
            ]
        left = jnp.concatenate([jnp.where(inside, g[0], 0.0) for g in groups], axis=0)
        empty = [jnp.zeros(shape, F32)] * len(wide)
        right = jnp.concatenate(
            [
                jnp.concatenate(done[g - first] if first <= g < last else empty, axis=1)
                for g in range(len(groups))
            ],
            axis=0,
        )
        change = product(left, right)
        for g in range(len(groups)):
            if first <= g < last:
                groups[g] = done[g - first]
            elif g in ahead:
                groups[g] = ahead[g]
            else:
                rows = change[8 * g : 8 * g + 8]
                groups[g] = [
                    x - rows[:, size * w : size * (w + 1)] for w, x in enumerate(kept(g))
                ]
    return [jnp.concatenate([g[w] for g in groups], axis=0) for w in range(len(wide))]


def solve_kernel(
    col_ref, gram_ref, basis_ref, residual_ref, out_ref, basis_out_ref, residual_out_ref
):
    basis_out_ref[...] = basis_ref[...]
    residual_out_ref[...] = residual_ref[...]
    dom_count, height, half = gram_ref.shape
    size = 2 * half
    rows = height - 1
    row, column = iota((half, half), 0), iota((half, half), 1)

    def block(start):
        return jnp.concatenate(
            [gram_ref[start // rows + k, :rows] for k in range(half // rows)], axis=0
        )

    spare = [gram_ref[index, rows:] for index in range(3)]
    square, cross = block(0), block(half)
    turned = square.T
    first = jnp.where(row <= column, square, turned)
    second = jnp.where(row < column, turned, jnp.where(row == column, spare[0], square))
    first_inverse, carried = eliminate(first, cross)
    second = second - dot_tn(cross, carried, HIGHEST)
    top = jnp.broadcast_to(spare[1], (8, half))
    x_top = dot_nn(top, first_inverse, HIGHEST)[:1]
    low = spare[2] - dot_nn(top, carried, HIGHEST)[:1]
    low = jnp.broadcast_to(low, (half, half)).T
    second_inverse, back = eliminate(second, -carried.T)
    x_bottom = jnp.sum(low * second_inverse, axis=0, keepdims=True)
    x_top = x_top + jnp.sum(low * back, axis=0, keepdims=True)
    width = out_ref.shape[1]
    out = jnp.zeros((1, width), F32)
    for index in range(size // width):
        mine = slice(index * width // 2, (index + 1) * width // 2)
        own = -jnp.concatenate([x_top[:, mine], x_bottom[:, mine]], axis=1)
        out = jnp.where(col_ref[0] == index, own, out)
    out_ref[...] = out


VMEM = pl.BlockSpec(memory_space=pltpu.VMEM)
SMEM = pl.BlockSpec(memory_space=pltpu.SMEM)
ANY = pl.BlockSpec(memory_space=pl.ANY)


def body(basis_panel, jacobian, neighbors, sample_rows, residual_parts):
    dom_count, col_count = lax.axis_size("dom"), lax.axis_size("col")
    col_index = lax.axis_index("col")
    width = basis_panel.shape[0]
    entries = sample_rows.shape[0]
    elements = neighbors.shape[0]
    node = jacobian.shape[1]
    size = width * col_count
    shape = jax.ShapeDtypeStruct
    reach = min(dom_count - 1, REACH_MOST)
    part = ROWS_DEV // col_count
    chunk = (size // dom_count + 1, size // 2)
    jacobian_basis, sampled_residual, whole = pl.pallas_call(
        functools.partial(step_kernel, dom_count, col_count, reach),
        out_shape=(
            pltpu.VMEM((width, ROWS_DEV), F32), pltpu.VMEM((1, ROWS_DEV), F32), pltpu.VMEM((dom_count,) + chunk, F32)
        ),
        in_specs=[ANY] * 5,
        out_specs=(VMEM, VMEM, VMEM),
        scratch_shapes=[
            pltpu.SMEM(neighbors.shape[::-1], jnp.int32),
            pltpu.VMEM((1, entries), jnp.int32),
            pltpu.VMEM((1, entries), F32),
            pltpu.VMEM(basis_panel.shape, BF16),
            pltpu.VMEM(jacobian.shape, BF16),
            pltpu.SemaphoreType.DMA((5,)),
            pltpu.VMEM((elements, width, -(-node // LANES) * LANES), BF16),
            pltpu.VMEM((2 * width + 32, entries), BF16),
            pltpu.VMEM((reach, width // 2 + 8, CAP), F32),
            pltpu.VMEM((reach, width // 2, CAP), F32),
            pltpu.VMEM((reach, width // 2 + 8, CAP), F32),
            pltpu.VMEM((reach, width // 2, CAP), F32),
            pltpu.VMEM((width + 8, ROWS_DEV), F32),
            pltpu.VMEM((entries, LANES), BF16),
            pltpu.VMEM((entries, LANES), BF16),
            pltpu.VMEM((width + 32, reach * CAP), BF16),
            pltpu.VMEM((width, reach * CAP), BF16),
            pltpu.VMEM((1, reach * CAP), jnp.int32),
            pltpu.VMEM((2, col_count, width // 2, part), F32),
            pltpu.VMEM((2, col_count, width // 2, part), F32),
            pltpu.VMEM((dom_count,) + chunk, F32),
            pltpu.VMEM((dom_count - 1,) + chunk, F32),
            pltpu.VMEM(chunk, F32),
            pltpu.VMEM((col_count - 1,) + chunk, F32),
            pltpu.VMEM(chunk, F32),
            pltpu.VMEM((dom_count,) + chunk, F32),
            pltpu.SemaphoreType.DMA((2, 2 * reach)),
            pltpu.SemaphoreType.DMA((2, 2 * (col_count - 1))),
            pltpu.SemaphoreType.DMA((2, dom_count - 1)),
            pltpu.SemaphoreType.DMA((2, col_count - 1)),
            pltpu.SemaphoreType.DMA((2, dom_count - 1)),
        ],
        compiler_params=pltpu.CompilerParams(
            collective_id=0, has_side_effects=True, vmem_limit_bytes=VMEM_BYTES
        ),
        name="step",
    )(
        neighbors.T,
        basis_panel,
        jacobian,
        sample_rows.reshape(1, entries),
        residual_parts.reshape(1, entries),
    )
    reduced_step, jacobian_basis, sampled_residual = pl.pallas_call(
        solve_kernel,
        out_shape=(
            shape((1, width), F32), shape((width, ROWS_DEV), F32), shape((1, ROWS_DEV), F32)
        ),
        in_specs=[SMEM, VMEM, VMEM, VMEM],
        out_specs=(VMEM, VMEM, VMEM),
        compiler_params=pltpu.CompilerParams(vmem_limit_bytes=VMEM_BYTES),
        name="solve",
    )(
        col_index.astype(jnp.int32).reshape(1),
        pltpu.with_memory_space_constraint(whole, pltpu.VMEM),
        pltpu.with_memory_space_constraint(jacobian_basis, pltpu.VMEM),
        pltpu.with_memory_space_constraint(sampled_residual, pltpu.VMEM),
    )
    return (jacobian_basis, sampled_residual[0], reduced_step[0])


def solution(mesh):
    placed = (P("col", "dom"), P(None, None, "dom"), P("dom", None), P("dom"), P("dom"))
    return jax.shard_map(
        body,
        mesh=mesh,
        in_specs=placed,
        out_specs=(P("col", "dom"), P("dom"), P("col")),
        check_vma=False,
    )
```

```python
import functools

import jax
import jax.numpy as jnp
from jax import lax
from jax.experimental import pallas as pl
from jax.experimental.pallas import tpu as pltpu
from jax.sharding import PartitionSpec as P

ROWS_DEV = 1024
CAP = 256
REACH_MOST = 8
LANES = 128
PIVOTS = 16
VMEM_BYTES = 62 * 2**20
HIGHEST = lax.Precision.HIGHEST
F32 = jnp.float32
BF16 = jnp.bfloat16


def iota(shape, dim):
    return lax.broadcasted_iota(jnp.int32, shape, dim)


def dot_nn(a, b, precision=None):
    return lax.dot_general(
        a, b, (((1,), (0,)), ((), ())), precision=precision, preferred_element_type=F32
    )


def dot_nt(a, b, precision=None):
    return lax.dot_general(
        a, b, (((1,), (1,)), ((), ())), precision=precision, preferred_element_type=F32
    )


def dot_tn(a, b, precision=None):
    return lax.dot_general(
        a, b, (((0,), (0,)), ((), ())), precision=precision, preferred_element_type=F32
    )


def split_values(x):
    high = x.astype(BF16)
    return high, (x - high.astype(F32)).astype(BF16)


def split_extra(x):
    high = x.astype(BF16).astype(F32)
    middle = (x - high).astype(BF16).astype(F32)
    low = x - high - middle
    return jnp.concatenate([high, middle, low, jnp.zeros_like(x)], axis=0).astype(BF16)


def join(found, width):
    values = found[:width] + found[width : 2 * width]
    base = 2 * width
    extra = found[base : base + 8] + found[base + 8 : base + 16] + found[base + 16 : base + 24]
    return jnp.concatenate([values, extra], axis=0)


def spread_places(places, height):
    turned = jnp.concatenate(
        [
            jnp.broadcast_to(places[:, k : k + LANES], (LANES, LANES)).T
            for k in range(0, height, LANES)
        ],
        axis=0,
    )
    tile = turned >> (CAP.bit_length() - 1)
    return tile.astype(F32).astype(BF16), (turned & (CAP - 1)).astype(F32).astype(BF16)


def pick(terms, tiles, spots, tile):
    wanted = jnp.asarray(tile, jnp.int32).astype(F32)
    near = jnp.where(tiles == jnp.full(tiles.shape, wanted, F32).astype(BF16), spots, -1.0)
    lanes = [
        (iota(tiles.shape, 1) + start).astype(F32).astype(BF16) for start in range(0, CAP, LANES)
    ]
    chosen = jnp.concatenate([jnp.where(near == lane, 1.0, 0.0) for lane in lanes], axis=1)
    return dot_nn(terms, chosen.astype(BF16))


def pick_turned(terms, targets, base):
    count = targets.shape[1]
    near = jnp.clip(targets - base, -1, CAP).astype(F32)
    near = jnp.broadcast_to(near, (16, count)).astype(BF16)
    near = jnp.concatenate([near] * (CAP // 16), axis=0)
    spots = iota((CAP, LANES), 0).astype(F32).astype(BF16)
    spots = jnp.concatenate([spots] * (count // LANES), axis=1)
    return dot_nt(terms, jnp.where(spots == near, 1.0, 0.0).astype(BF16))


def fold(value, count):
    return jnp.where(value >= count, value - count, value)


def step_kernel(
    dom_count, col_count, reach,
    links_hbm, panel_hbm, blocks_hbm, rows_hbm, parts_hbm,
    basis_ref, residual_ref, gram_ref, inverse_ref,
    links_ref, rows_ref, parts_ref, panel_ref, blocks_ref, load_sems, panels, terms,
    send, send_late, arrived, arrived_late, local, tiles_held, spots_held,
    terms_in, terms_late, landing, pieces, others,
    parts, landed, mine, lines, total, whole,
    late_parts, late_landed, late_mine, late_lines, late_total, late_whole,
    dom_sems, col_sems, part_sems, line_sems, whole_sems,
):
    dom, col = lax.axis_index("dom"), lax.axis_index("col")
    width = panel_ref.shape[0]
    coupled_count, node, entries = blocks_ref.shape
    elements = links_ref.shape[1]
    rs = entries // elements
    group = LANES // rs
    part = ROWS_DEV // col_count
    size = width * col_count
    half_width = width // 2

    def remote(source, target, sems, index, device):
        return pltpu.make_async_remote_copy(
            src_ref=source,
            dst_ref=target,
            send_sem=sems.at[0, index],
            recv_sem=sems.at[1, index],
            device_id=device,
            device_id_type=pl.DeviceIdType.MESH,
        )

    def dom_at(o):
        return fold(dom + o, dom_count), col

    def col_at(o):
        return dom, fold(col + o, col_count)

    def offset_at(turn):
        if reach != dom_count - 1 or dom_count & reach:
            return turn + 1
        flips = jnp.where(turn < reach - 1, reach - 1 - turn // 2 * 2 + turn % 2, 1)
        partner, bit = 0, 1
        while bit < dom_count:
            partner = partner + (dom // bit + flips // bit) % 2 * bit
            bit *= 2
        return (dom_count + partner - dom) % dom_count

    def dom_copy(half, o):
        source, target = ((send, arrived), (send_late, arrived_late))[half]
        return remote(source.at[o - 1], target.at[o - 1], dom_sems, half * reach + o - 1, dom_at(o))

    def col_copy(half, o):
        there = fold(col + o, col_count)
        return remote(
            pieces.at[half, there], others.at[half, col],
            col_sems, half * (col_count - 1) + o - 1, col_at(o),
        )

    def part_copy(late, o):
        source, target = ((parts, landed), (late_parts, late_landed))[late]
        place = late * (dom_count - 1) + o - 1
        there = fold(dom + o, dom_count)
        return remote(source.at[there], target.at[o - 1], part_sems, place, dom_at(o))

    def line_copy(late, o):
        source, target = ((mine, lines), (late_mine, late_lines))[late]
        place = late * (col_count - 1) + o - 1
        return remote(source, target.at[o - 1], line_sems, place, col_at(o))

    def whole_copy(late, o):
        source, target = ((total, whole), (late_total, late_whole))[late]
        place = late * (dom_count - 1) + o - 1
        return remote(source, target.at[dom], whole_sems, place, dom_at(o))

    panel_load = pltpu.make_async_copy(panel_hbm, panel_ref, load_sems.at[0])
    blocks_load = pltpu.make_async_copy(blocks_hbm, blocks_ref, load_sems.at[1])
    small_loads = [
        pltpu.make_async_copy(rows_hbm, rows_ref, load_sems.at[2]),
        pltpu.make_async_copy(parts_hbm, parts_ref, load_sems.at[3]),
        pltpu.make_async_copy(links_hbm, links_ref, load_sems.at[4]),
    ]
    for load in small_loads:
        load.start()
    panel_load.start()
    blocks_load.start()
    barrier = pltpu.get_barrier_semaphore()

    for count, device_at in ((dom_count, dom_at), (col_count, col_at)):

        @pl.loop(1, count)
        def _(o, device_at=device_at):
            pl.semaphore_signal(
                barrier, inc=1, device_id=device_at(o), device_id_type=pl.DeviceIdType.MESH
            )

    for load in small_loads:
        load.wait()
    shift = ROWS_DEV.bit_length() - 1
    match_rows = max(16, dom_count)
    before = (iota((LANES, LANES), 0) < iota((LANES, LANES), 1)).astype(F32).astype(BF16)
    carry = jnp.zeros((match_rows, 1), F32)
    targets = []
    for start in range(0, entries, LANES):
        rows = rows_ref[:, start : start + LANES]
        offset = fold((rows >> shift) - dom + dom_count, dom_count)
        local_row = rows & (ROWS_DEV - 1)
        matches = (iota((match_rows, LANES), 0) == offset).astype(F32)
        ranks = jnp.sum(
            matches * (dot_nn(matches.astype(BF16), before) + carry), axis=0, keepdims=True
        ).astype(jnp.int32)
        carry = carry + jnp.sum(matches, axis=1, keepdims=True)
        targets.append(
            jnp.where(offset == 0, local_row, ROWS_DEV + (offset - 1) * CAP + ranks)
        )
    targets = jnp.concatenate(targets, axis=1)
    tiles_held[...], spots_held[...] = spread_places(targets, entries)

    row_values = (rows_ref[...] & (ROWS_DEV - 1)).astype(F32)
    which = iota((8, entries), 0)
    extra = jnp.where(which == 0, parts_ref[...], jnp.where(which == 1, row_values, 0.0))
    terms[2 * width :, :] = split_extra(extra)

    deep = panels.shape[2]
    no_columns = jnp.zeros((width, deep - node), BF16)
    no_rows = jnp.zeros((deep - node, LANES), BF16)
    panel_load.wait()

    @pl.loop(0, elements // 2, unroll=4)
    def _(pair):
        window = panel_ref[:, pl.ds(pl.multiple_of(pair * 2 * node, LANES), 2 * node)]
        for which in range(2):
            held = window[:, which * node : (which + 1) * node]
            panels[2 * pair + which] = jnp.concatenate([held, no_columns], axis=1)

    lane_element = iota((width, LANES), 1) // rs

    blocks_load.wait()

    @pl.loop(0, elements // group, unroll=16)
    def _(block):
        columns = pl.ds(pl.multiple_of(block * LANES, LANES), LANES)
        picked = jnp.concatenate(
            [
                jnp.concatenate(
                    [panels[links_ref[coupled, block * group + q]] for q in range(group)], axis=0
                )
                for coupled in range(coupled_count)
            ],
            axis=1,
        )
        against = []
        for coupled in range(coupled_count):
            against += [blocks_ref[coupled, :, columns], no_rows]
        found = dot_nn(picked, jnp.concatenate(against, axis=0))
        out = found[:width]
        for q in range(1, group):
            out = jnp.where(lane_element == q, found[q * width : (q + 1) * width], out)
        high, low = split_values(out)
        terms[:width, columns] = high
        terms[width : 2 * width, columns] = low

    pl.semaphore_wait(barrier, dom_count + col_count - 2)

    @pl.loop(0, reach)
    def _(turn):
        o = offset_at(turn)
        found = join(pick(terms[...], tiles_held[...], spots_held[...], ROWS_DEV // CAP + o - 1), width)
        send[o - 1, :half_width] = found[:half_width]
        send[o - 1, half_width:] = found[width:]
        send_late[o - 1] = found[half_width:width]
        dom_copy(0, o).start()

    @pl.loop(0, reach)
    def _(turn):
        dom_copy(1, offset_at(turn)).start()

    @pl.loop(0, ROWS_DEV // CAP)
    def _(tile):
        base = tile * CAP
        local[:, pl.ds(pl.multiple_of(base, CAP), CAP)] = join(
            pick(terms[...], tiles_held[...], spots_held[...], tile), width
        )

    def assemble(half, base):
        columns = pl.ds(pl.multiple_of(base, CAP), CAP)
        found = pick_turned((terms_in, terms_late)[half][...], landing[...], base)
        start = half * half_width
        values = found[:half_width] + found[half_width : 2 * half_width]
        values = values + local[start : start + half_width, columns]
        basis_ref[start : start + half_width, columns] = values
        if half == 0:
            extra = found[2 * half_width :]
            extra = extra[:8] + extra[8:16] + extra[16:24] + local[width:, columns]
            residual_ref[:, columns] = extra[:1]
        return values

    def pass_on(half):
        if part == CAP:

            @pl.loop(1, col_count)
            def _(o):
                there = fold(col + o, col_count)
                pieces[half, there] = assemble(half, there * part)
                col_copy(half, o).start()

            others[half, col] = assemble(half, col * part)
            return
        for tile in range(ROWS_DEV // CAP):
            assemble(half, tile * CAP)
        rows = slice(half * half_width, (half + 1) * half_width)
        for index in range(col_count):
            pieces[half, index] = basis_ref[rows, index * part : (index + 1) * part]

        @pl.loop(1, col_count)
        def _(o):
            col_copy(half, o).start()

        others[half, col] = pieces[half, col]

    for o in range(1, reach + 1):
        dom_copy(0, o).wait_recv()
        columns = slice((o - 1) * CAP, o * CAP)
        block = arrived[o - 1]
        extra = block[half_width:]
        high, low = split_values(block[:half_width])
        terms_in[:, columns] = jnp.concatenate([high, low, split_extra(extra)], axis=0)
        landing[:, columns] = extra[1:2].astype(jnp.int32)

    pass_on(0)
    own_residual = jnp.zeros((1, part), F32)
    for index in range(col_count):
        piece = residual_ref[:, index * part : (index + 1) * part]
        own_residual = own_residual + jnp.where(index == col, piece, 0.0)

    for o in range(1, reach + 1):
        dom_copy(1, o).wait_recv()
        high, low = split_values(arrived_late[o - 1])
        terms_late[:, (o - 1) * CAP : o * CAP] = jnp.concatenate([high, low], axis=0)

    pass_on(1)
    half = size // 2
    rows = half // dom_count

    def exchange(copy, late, count):
        @pl.loop(1, count)
        def _(o):
            copy(late, o).start()

    def finish(copy, late, count):
        @pl.loop(1, count)
        def _(o):
            copy(late, o).wait_recv()

    for o in range(1, col_count):
        col_copy(0, o).wait_recv()
    top = others[0].reshape(half, part)
    first = dot_nt(top, top, HIGHEST)
    for index in range(dom_count):
        parts[index] = first[index * rows : (index + 1) * rows]
    exchange(part_copy, 0, dom_count)
    for o in range(1, col_count):
        col_copy(1, o).wait_recv()
    bottom = others[1].reshape(half, part)
    cross = dot_nt(top, bottom, HIGHEST)
    second = dot_nt(bottom, bottom, HIGHEST)
    residual = jnp.broadcast_to(own_residual, (8, part))
    spare = [dot_nt(residual, block, HIGHEST)[:1] for block in (top, bottom)]
    packed = jnp.concatenate([cross, second], axis=0)
    for index in range(dom_count):
        late_parts[index, : 2 * rows] = packed[index * 2 * rows : (index + 1) * 2 * rows]
        late_parts[index, 2 * rows :] = spare[index] if index < 2 else jnp.zeros((1, half), F32)
    exchange(part_copy, 1, dom_count)
    finish(part_copy, 0, dom_count)
    mine[...] = jnp.sum(landed[...], axis=0) + parts[dom]
    exchange(line_copy, 0, col_count)
    finish(part_copy, 1, dom_count)
    late_mine[...] = jnp.sum(late_landed[...], axis=0) + late_parts[dom]
    exchange(line_copy, 1, col_count)
    finish(line_copy, 0, col_count)
    total[...] = jnp.sum(lines[...], axis=0) + mine[...]
    exchange(whole_copy, 0, dom_count)
    whole[dom] = total[...]
    finish(line_copy, 1, col_count)
    late_total[...] = jnp.sum(late_lines[...], axis=0) + late_mine[...]
    exchange(whole_copy, 1, dom_count)
    late_whole[dom] = late_total[...]
    finish(whole_copy, 0, dom_count)
    first = jnp.concatenate([whole[index] for index in range(dom_count)], axis=0)
    inverse_ref[...] = eliminate([first])[0]
    finish(whole_copy, 1, dom_count)
    gram_ref[...] = late_whole[...]

    @pl.loop(1, reach + 1)
    def _(o):
        for late in range(2):
            dom_copy(late, o).wait_send()

    @pl.loop(1, col_count)
    def _(o):
        for late in range(2):
            col_copy(late, o).wait_send()
            line_copy(late, o).wait_send()

    @pl.loop(1, dom_count)
    def _(o):
        for late in range(2):
            part_copy(late, o).wait_send()
            whole_copy(late, o).wait_send()


def tree_sum(terms):
    while len(terms) > 1:
        odd = [terms[-1]] if len(terms) % 2 else []
        terms = [a + b for a, b in zip(terms[::2], terms[1::2])] + odd
    return terms[0]


def split_three(x):
    high = x.astype(BF16)
    rest = x - high.astype(F32)
    middle = rest.astype(BF16)
    return high, middle, (rest - middle.astype(F32)).astype(BF16)


def product(a, b):
    ah, am, al = split_three(a)
    bh, bm, bl = split_three(b)

    def pair(a1, b1, a2, b2):
        return dot_nn(
            jnp.concatenate([a1, a2], axis=1), jnp.concatenate([b1, b2], axis=0)
        )

    return pair(ah, bh, am, bh) + (pair(ah, bm, am, bm) + pair(ah, bl, al, bh))


def eliminate(wide):
    size = wide[0].shape[0]
    shape = (PIVOTS, size)
    row, lane = iota(shape, 0), iota(shape, 1)
    blocks = [[w[k : k + PIVOTS] for w in wide] for k in range(0, size, PIVOTS)]

    def columns_of(block, start):
        return [
            jnp.broadcast_to(block[:, start + j : start + j + 1], shape) for j in range(PIVOTS)
        ]

    for turn, panel in enumerate(blocks):
        start = turn * PIVOTS
        inside = (lane >= start) & (lane < start + PIVOTS)
        columns = jnp.stack(columns_of(panel[0], start))
        first = jnp.where(inside, (lane - start == row).astype(F32), panel[0])
        work = jnp.stack([first] + panel[1:])
        scales = jnp.zeros(shape, F32)
        for i in range(PIVOTS):
            here = row == i
            column = columns[0]
            scale = 1.0 / jnp.broadcast_to(column[i : i + 1], shape)
            factor = jnp.where(here, 0.0, column * scale)
            scales = jnp.where(here, scale, scales)
            if i + 1 < PIVOTS:
                columns = columns[1:]
                columns = columns - factor * columns[:, i : i + 1]
            work = work - factor * work[:, i : i + 1]
        work = work * scales
        done = [work[w] for w in range(len(wide))]

        def kept(block):
            return [jnp.where(inside, 0.0, block[0])] + block[1:]

        ahead = None
        if turn + 1 < len(blocks):
            block = blocks[turn + 1]
            held = columns_of(block[0], start)
            ahead = [
                x - tree_sum([held[k] * done[w][k : k + 1] for k in range(PIVOTS)])
                for w, x in enumerate(kept(block))
            ]
        left = jnp.concatenate([jnp.where(inside, b[0], 0.0) for b in blocks], axis=0)
        empty = jnp.zeros((PIVOTS, size * len(wide)), F32)
        right = [empty] * len(blocks)
        right[turn] = jnp.concatenate(done, axis=1)
        change = product(left, jnp.concatenate(right, axis=0))
        for k, block in enumerate(blocks):
            if k == turn:
                blocks[k] = done
            elif k == turn + 1:
                blocks[k] = ahead
            else:
                rows = change[k * PIVOTS : (k + 1) * PIVOTS]
                blocks[k] = [
                    x - rows[:, size * w : size * (w + 1)] for w, x in enumerate(kept(block))
                ]
    return [jnp.concatenate([b[w] for b in blocks], axis=0) for w in range(len(wide))]


def solve_kernel(
    col_ref, gram_ref, inverse_ref, basis_ref, residual_ref, out_ref, basis_out_ref, residual_out_ref, sems
):
    copies = [
        pltpu.make_async_copy(basis_ref, basis_out_ref, sems.at[0]),
        pltpu.make_async_copy(residual_ref, residual_out_ref, sems.at[1]),
    ]
    for copy in copies:
        copy.start()
    dom_count, height, half = gram_ref.shape
    size = 2 * half
    rows = height - 1

    def block(start):
        return jnp.concatenate(
            [gram_ref[start // rows + k, :rows] for k in range(half // rows)], axis=0
        )

    spare = [gram_ref[index, rows:] for index in range(2)]
    cross, second = block(0), block(half)
    first_inverse = inverse_ref[...]
    carried = product(first_inverse, cross)
    second = second - dot_tn(cross, carried, HIGHEST)
    top = jnp.broadcast_to(spare[0], (8, half))
    x_top = dot_nn(top, first_inverse, HIGHEST)[:1]
    low = spare[1] - dot_nn(top, carried, HIGHEST)[:1]
    low = jnp.broadcast_to(low, (half, half)).T
    second_inverse, back = eliminate([second, -carried.T])
    x_bottom = jnp.sum(low * second_inverse, axis=0, keepdims=True)
    x_top = x_top + jnp.sum(low * back, axis=0, keepdims=True)
    width = out_ref.shape[1]
    out = jnp.zeros((1, width), F32)
    for index in range(size // width):
        mine = slice(index * width // 2, (index + 1) * width // 2)
        own = -jnp.concatenate([x_top[:, mine], x_bottom[:, mine]], axis=1)
        out = jnp.where(col_ref[0] == index, own, out)
    out_ref[...] = out
    for copy in copies:
        copy.wait()


VMEM = pl.BlockSpec(memory_space=pltpu.VMEM)
SMEM = pl.BlockSpec(memory_space=pltpu.SMEM)
ANY = pl.BlockSpec(memory_space=pl.ANY)


def body(basis_panel, jacobian, neighbors, sample_rows, residual_parts):
    dom_count, col_count = lax.axis_size("dom"), lax.axis_size("col")
    col_index = lax.axis_index("col")
    width = basis_panel.shape[0]
    entries = sample_rows.shape[0]
    elements = neighbors.shape[0]
    node = jacobian.shape[1]
    size = width * col_count
    shape = jax.ShapeDtypeStruct
    reach = min(dom_count - 1, REACH_MOST)
    part = ROWS_DEV // col_count
    early = (size // 2 // dom_count, size // 2)
    chunk = (size // dom_count + 1, size // 2)
    jacobian_basis, sampled_residual, whole, inverse = pl.pallas_call(
        functools.partial(step_kernel, dom_count, col_count, reach),
        out_shape=(
            pltpu.VMEM((width, ROWS_DEV), F32), pltpu.VMEM((1, ROWS_DEV), F32), pltpu.VMEM((dom_count,) + chunk, F32), pltpu.VMEM((size // 2, size // 2), F32)
        ),
        in_specs=[ANY] * 5,
        out_specs=(VMEM, VMEM, VMEM, VMEM),
        scratch_shapes=[
            pltpu.SMEM(neighbors.shape[::-1], jnp.int32),
            pltpu.VMEM((1, entries), jnp.int32),
            pltpu.VMEM((1, entries), F32),
            pltpu.VMEM(basis_panel.shape, BF16),
            pltpu.VMEM(jacobian.shape, BF16),
            pltpu.SemaphoreType.DMA((5,)),
            pltpu.VMEM((elements, width, -(-node // LANES) * LANES), BF16),
            pltpu.VMEM((2 * width + 32, entries), BF16),
            pltpu.VMEM((reach, width // 2 + 8, CAP), F32),
            pltpu.VMEM((reach, width // 2, CAP), F32),
            pltpu.VMEM((reach, width // 2 + 8, CAP), F32),
            pltpu.VMEM((reach, width // 2, CAP), F32),
            pltpu.VMEM((width + 8, ROWS_DEV), F32),
            pltpu.VMEM((entries, LANES), BF16),
            pltpu.VMEM((entries, LANES), BF16),
            pltpu.VMEM((width + 32, reach * CAP), BF16),
            pltpu.VMEM((width, reach * CAP), BF16),
            pltpu.VMEM((1, reach * CAP), jnp.int32),
            pltpu.VMEM((2, col_count, width // 2, part), F32),
            pltpu.VMEM((2, col_count, width // 2, part), F32),
            pltpu.VMEM((dom_count,) + early, F32),
            pltpu.VMEM((dom_count - 1,) + early, F32),
            pltpu.VMEM(early, F32),
            pltpu.VMEM((col_count - 1,) + early, F32),
            pltpu.VMEM(early, F32),
            pltpu.VMEM((dom_count,) + early, F32),
            pltpu.VMEM((dom_count,) + chunk, F32),
            pltpu.VMEM((dom_count - 1,) + chunk, F32),
            pltpu.VMEM(chunk, F32),
            pltpu.VMEM((col_count - 1,) + chunk, F32),
            pltpu.VMEM(chunk, F32),
            pltpu.VMEM((dom_count,) + chunk, F32),
            pltpu.SemaphoreType.DMA((2, 2 * reach)),
            pltpu.SemaphoreType.DMA((2, 2 * (col_count - 1))),
            pltpu.SemaphoreType.DMA((2, 2 * (dom_count - 1))),
            pltpu.SemaphoreType.DMA((2, 2 * (col_count - 1))),
            pltpu.SemaphoreType.DMA((2, 2 * (dom_count - 1))),
        ],
        compiler_params=pltpu.CompilerParams(
            collective_id=0, has_side_effects=True, vmem_limit_bytes=VMEM_BYTES
        ),
        name="step",
    )(
        neighbors.T,
        basis_panel,
        jacobian,
        sample_rows.reshape(1, entries),
        residual_parts.reshape(1, entries),
    )
    reduced_step, jacobian_basis, sampled_residual = pl.pallas_call(
        solve_kernel,
        out_shape=(
            shape((1, width), F32), shape((width, ROWS_DEV), F32), shape((1, ROWS_DEV), F32)
        ),
        in_specs=[SMEM, VMEM, VMEM, VMEM, VMEM],
        out_specs=(VMEM, ANY, ANY),
        scratch_shapes=[pltpu.SemaphoreType.DMA((2,))],
        compiler_params=pltpu.CompilerParams(vmem_limit_bytes=VMEM_BYTES),
        name="solve",
    )(
        col_index.astype(jnp.int32).reshape(1),
        pltpu.with_memory_space_constraint(whole, pltpu.VMEM),
        pltpu.with_memory_space_constraint(inverse, pltpu.VMEM),
        pltpu.with_memory_space_constraint(jacobian_basis, pltpu.VMEM),
        pltpu.with_memory_space_constraint(sampled_residual, pltpu.VMEM),
    )
    return (jacobian_basis, sampled_residual[0], reduced_step[0])


def solution(mesh):
    placed = (P("col", "dom"), P(None, None, "dom"), P("dom", None), P("dom"), P("dom"))
    return jax.shard_map(
        body,
        mesh=mesh,
        in_specs=placed,
        out_specs=(P("col", "dom"), P("dom"), P("col")),
        check_vma=False,
    )
```

```python
import functools

import jax
import jax.numpy as jnp
from jax import lax
from jax.experimental import pallas as pl
from jax.experimental.pallas import tpu as pltpu
from jax.sharding import PartitionSpec as P

ROWS_DEV = 1024
CAP = 256
REACH_MOST = 8
LANES = 128
PIVOTS = 16
LOADS = 2
VMEM_BYTES = 62 * 2**20
HIGHEST = lax.Precision.HIGHEST
F32 = jnp.float32
BF16 = jnp.bfloat16


def iota(shape, dim):
    return lax.broadcasted_iota(jnp.int32, shape, dim)


def dot_nn(a, b, precision=None):
    return lax.dot_general(
        a, b, (((1,), (0,)), ((), ())), precision=precision, preferred_element_type=F32
    )


def dot_nt(a, b, precision=None):
    return lax.dot_general(
        a, b, (((1,), (1,)), ((), ())), precision=precision, preferred_element_type=F32
    )


def dot_tn(a, b, precision=None):
    return lax.dot_general(
        a, b, (((0,), (0,)), ((), ())), precision=precision, preferred_element_type=F32
    )


def split_values(x):
    high = x.astype(BF16)
    return high, (x - high.astype(F32)).astype(BF16)


def split_extra(x):
    high = x.astype(BF16).astype(F32)
    middle = (x - high).astype(BF16).astype(F32)
    low = x - high - middle
    return jnp.concatenate([high, middle, low, jnp.zeros_like(x)], axis=0).astype(BF16)


def join(found, width):
    values = found[:width] + found[width : 2 * width]
    base = 2 * width
    extra = found[base : base + 8] + found[base + 8 : base + 16] + found[base + 16 : base + 24]
    return jnp.concatenate([values, extra], axis=0)


def spread_places(places, height):
    turned = jnp.concatenate(
        [
            jnp.broadcast_to(places[:, k : k + LANES], (LANES, LANES)).T
            for k in range(0, height, LANES)
        ],
        axis=0,
    )
    tile = turned >> (CAP.bit_length() - 1)
    return tile.astype(F32).astype(BF16), (turned & (CAP - 1)).astype(F32).astype(BF16)


def pick(terms, tiles, spots, tile):
    wanted = jnp.asarray(tile, jnp.int32).astype(F32)
    near = jnp.where(tiles == jnp.full(tiles.shape, wanted, F32).astype(BF16), spots, -1.0)
    lanes = [
        (iota(tiles.shape, 1) + start).astype(F32).astype(BF16) for start in range(0, CAP, LANES)
    ]
    chosen = jnp.concatenate([jnp.where(near == lane, 1.0, 0.0) for lane in lanes], axis=1)
    return dot_nn(terms, chosen.astype(BF16))


def pick_turned(terms, targets, base):
    count = targets.shape[1]
    near = jnp.clip(targets - base, -1, CAP).astype(F32)
    near = jnp.broadcast_to(near, (16, count)).astype(BF16)
    near = jnp.concatenate([near] * (CAP // 16), axis=0)
    spots = iota((CAP, LANES), 0).astype(F32).astype(BF16)
    spots = jnp.concatenate([spots] * (count // LANES), axis=1)
    return dot_nt(terms, jnp.where(spots == near, 1.0, 0.0).astype(BF16))


def fold(value, count):
    return jnp.where(value >= count, value - count, value)


def step_kernel(
    dom_count, col_count, reach,
    links_hbm, panel_hbm, blocks_hbm, rows_hbm, parts_hbm,
    basis_ref, residual_ref, gram_ref, inverse_ref,
    links_ref, rows_ref, parts_ref, panel_ref, blocks_ref, load_sems, panels, terms,
    send, send_late, arrived, arrived_late, local, tiles_held, spots_held,
    terms_in, terms_late, landing, pieces, others,
    parts, landed, mine, lines, total, whole,
    late_parts, late_landed, late_mine, late_lines, late_total, late_whole,
    dom_sems, col_sems, part_sems, line_sems, whole_sems,
):
    dom, col = lax.axis_index("dom"), lax.axis_index("col")
    width = panel_ref.shape[0]
    coupled_count, node, entries = blocks_ref.shape
    elements = links_ref.shape[1]
    rs = entries // elements
    group = LANES // rs
    part = ROWS_DEV // col_count
    size = width * col_count
    half_width = width // 2

    def remote(source, target, sems, index, device):
        return pltpu.make_async_remote_copy(
            src_ref=source,
            dst_ref=target,
            send_sem=sems.at[0, index],
            recv_sem=sems.at[1, index],
            device_id=device,
            device_id_type=pl.DeviceIdType.MESH,
        )

    def dom_at(o):
        return fold(dom + o, dom_count), col

    def col_at(o):
        return dom, fold(col + o, col_count)

    def offset_at(turn):
        if reach != dom_count - 1 or dom_count & reach:
            return turn + 1
        flips = jnp.where(turn < reach - 1, reach - 1 - turn // 2 * 2 + turn % 2, 1)
        partner, bit = 0, 1
        while bit < dom_count:
            partner = partner + (dom // bit + flips // bit) % 2 * bit
            bit *= 2
        return (dom_count + partner - dom) % dom_count

    def dom_copy(half, o):
        source, target = ((send, arrived), (send_late, arrived_late))[half]
        return remote(source.at[o - 1], target.at[o - 1], dom_sems, half * reach + o - 1, dom_at(o))

    def col_copy(half, o):
        there = fold(col + o, col_count)
        return remote(
            pieces.at[half, there], others.at[half, col],
            col_sems, half * (col_count - 1) + o - 1, col_at(o),
        )

    def part_copy(late, o):
        source, target = ((parts, landed), (late_parts, late_landed))[late]
        place = late * (dom_count - 1) + o - 1
        there = fold(dom + o, dom_count)
        return remote(source.at[there], target.at[o - 1], part_sems, place, dom_at(o))

    def line_copy(late, o):
        source, target = ((mine, lines), (late_mine, late_lines))[late]
        place = late * (col_count - 1) + o - 1
        return remote(source, target.at[o - 1], line_sems, place, col_at(o))

    def whole_copy(late, o):
        source, target = ((total, whole), (late_total, late_whole))[late]
        place = late * (dom_count - 1) + o - 1
        return remote(source, target.at[dom], whole_sems, place, dom_at(o))

    def panel_load(k):
        share = elements // LOADS * node
        place = slice(k * share, (k + 1) * share)
        return pltpu.make_async_copy(
            panel_hbm.at[:, place], panel_ref.at[:, place], load_sems.at[3 + k]
        )

    def blocks_load(k):
        share = entries // LOADS
        place = slice(k * share, (k + 1) * share)
        return pltpu.make_async_copy(
            blocks_hbm.at[:, :, place], blocks_ref.at[:, :, place], load_sems.at[3 + LOADS + k]
        )

    small_loads = [
        pltpu.make_async_copy(rows_hbm, rows_ref, load_sems.at[0]),
        pltpu.make_async_copy(parts_hbm, parts_ref, load_sems.at[1]),
        pltpu.make_async_copy(links_hbm, links_ref, load_sems.at[2]),
    ]
    for load in small_loads:
        load.start()
    for k in range(LOADS):
        panel_load(k).start()
    for k in range(LOADS):
        blocks_load(k).start()
    barrier = pltpu.get_barrier_semaphore()

    for count, device_at in ((dom_count, dom_at), (col_count, col_at)):

        @pl.loop(1, count)
        def _(o, device_at=device_at):
            pl.semaphore_signal(
                barrier, inc=1, device_id=device_at(o), device_id_type=pl.DeviceIdType.MESH
            )

    for load in small_loads:
        load.wait()
    shift = ROWS_DEV.bit_length() - 1
    match_rows = max(16, dom_count)
    before = (iota((LANES, LANES), 0) < iota((LANES, LANES), 1)).astype(F32).astype(BF16)
    carry = jnp.zeros((match_rows, 1), F32)
    targets = []
    for start in range(0, entries, LANES):
        rows = rows_ref[:, start : start + LANES]
        offset = fold((rows >> shift) - dom + dom_count, dom_count)
        local_row = rows & (ROWS_DEV - 1)
        matches = (iota((match_rows, LANES), 0) == offset).astype(F32)
        ranks = jnp.sum(
            matches * (dot_nn(matches.astype(BF16), before) + carry), axis=0, keepdims=True
        ).astype(jnp.int32)
        carry = carry + jnp.sum(matches, axis=1, keepdims=True)
        targets.append(
            jnp.where(offset == 0, local_row, ROWS_DEV + (offset - 1) * CAP + ranks)
        )
    targets = jnp.concatenate(targets, axis=1)
    tiles_held[...], spots_held[...] = spread_places(targets, entries)

    row_values = (rows_ref[...] & (ROWS_DEV - 1)).astype(F32)
    which = iota((8, entries), 0)
    extra = jnp.where(which == 0, parts_ref[...], jnp.where(which == 1, row_values, 0.0))
    terms[2 * width :, :] = split_extra(extra)

    deep = panels.shape[2]
    no_columns = jnp.zeros((width, deep - node), BF16)
    no_rows = jnp.zeros((deep - node, LANES), BF16)
    pairs = elements // 2 // LOADS
    for k in range(LOADS):
        panel_load(k).wait()

        @pl.loop(k * pairs, (k + 1) * pairs, unroll=8)
        def _(pair):
            window = panel_ref[:, pl.ds(pl.multiple_of(pair * 2 * node, LANES), 2 * node)]
            for which in range(2):
                held = window[:, which * node : (which + 1) * node]
                panels[2 * pair + which] = jnp.concatenate([held, no_columns], axis=1)

    lane_element = iota((width, LANES), 1) // rs

    shares = elements // group // LOADS
    for k in range(LOADS):
        blocks_load(k).wait()

        @pl.loop(k * shares, (k + 1) * shares, unroll=shares)
        def _(block):
            columns = pl.ds(pl.multiple_of(block * LANES, LANES), LANES)
            picked = jnp.concatenate(
                [
                    jnp.concatenate(
                        [panels[links_ref[coupled, block * group + q]] for q in range(group)], axis=0
                    )
                    for coupled in range(coupled_count)
                ],
                axis=1,
            )
            against = []
            for coupled in range(coupled_count):
                against += [blocks_ref[coupled, :, columns], no_rows]
            found = dot_nn(picked, jnp.concatenate(against, axis=0))
            out = found[:width]
            for q in range(1, group):
                out = jnp.where(lane_element == q, found[q * width : (q + 1) * width], out)
            high, low = split_values(out)
            terms[:width, columns] = high
            terms[width : 2 * width, columns] = low

    pl.semaphore_wait(barrier, dom_count + col_count - 2)

    @pl.loop(0, reach)
    def _(turn):
        o = offset_at(turn)
        found = join(pick(terms[...], tiles_held[...], spots_held[...], ROWS_DEV // CAP + o - 1), width)
        send[o - 1, :half_width] = found[:half_width]
        send[o - 1, half_width:] = found[width : width + 2]
        send_late[o - 1] = found[half_width:width]
        dom_copy(0, o).start()

    @pl.loop(0, reach)
    def _(turn):
        dom_copy(1, offset_at(turn)).start()

    @pl.loop(0, ROWS_DEV // CAP)
    def _(tile):
        base = tile * CAP
        local[:, pl.ds(pl.multiple_of(base, CAP), CAP)] = join(
            pick(terms[...], tiles_held[...], spots_held[...], tile), width
        )

    def assemble(half, base):
        columns = pl.ds(pl.multiple_of(base, CAP), CAP)
        found = pick_turned((terms_in, terms_late)[half][...], landing[...], base)
        start = half * half_width
        values = found[:half_width] + found[half_width : 2 * half_width]
        values = values + local[start : start + half_width, columns]
        basis_ref[start : start + half_width, columns] = values
        if half == 0:
            extra = found[2 * half_width :]
            extra = extra[:8] + extra[8:16] + extra[16:24] + local[width:, columns]
            residual_ref[:, columns] = extra[:1]
        return values

    def pass_on(half):
        if part == CAP:

            @pl.loop(1, col_count)
            def _(o):
                there = fold(col + o, col_count)
                pieces[half, there] = assemble(half, there * part)
                col_copy(half, o).start()

            others[half, col] = assemble(half, col * part)
            return
        for tile in range(ROWS_DEV // CAP):
            assemble(half, tile * CAP)
        rows = slice(half * half_width, (half + 1) * half_width)
        for index in range(col_count):
            pieces[half, index] = basis_ref[rows, index * part : (index + 1) * part]

        @pl.loop(1, col_count)
        def _(o):
            col_copy(half, o).start()

        others[half, col] = pieces[half, col]

    for o in range(1, reach + 1):
        dom_copy(0, o).wait_recv()
        columns = slice((o - 1) * CAP, o * CAP)
        block = arrived[o - 1]
        extra = jnp.concatenate([block[half_width:], jnp.zeros((6, CAP), F32)], axis=0)
        high, low = split_values(block[:half_width])
        terms_in[:, columns] = jnp.concatenate([high, low, split_extra(extra)], axis=0)
        landing[:, columns] = extra[1:2].astype(jnp.int32)

    pass_on(0)
    own_residual = jnp.zeros((1, part), F32)
    for index in range(col_count):
        piece = residual_ref[:, index * part : (index + 1) * part]
        own_residual = own_residual + jnp.where(index == col, piece, 0.0)

    for o in range(1, reach + 1):
        dom_copy(1, o).wait_recv()
        high, low = split_values(arrived_late[o - 1])
        terms_late[:, (o - 1) * CAP : o * CAP] = jnp.concatenate([high, low], axis=0)

    pass_on(1)
    half = size // 2
    rows = half // dom_count

    def exchange(copy, late, count):
        @pl.loop(1, count)
        def _(o):
            copy(late, o).start()

    def finish(copy, late, count):
        @pl.loop(1, count)
        def _(o):
            copy(late, o).wait_recv()

    for o in range(1, col_count):
        col_copy(0, o).wait_recv()
    top = others[0].reshape(half, part)
    first = dot_nt(top, top, HIGHEST)
    for index in range(dom_count):
        parts[index] = first[index * rows : (index + 1) * rows]
    exchange(part_copy, 0, dom_count)
    for o in range(1, col_count):
        col_copy(1, o).wait_recv()
    bottom = others[1].reshape(half, part)
    tall = jnp.concatenate([bottom, jnp.broadcast_to(own_residual, (8, part))], axis=0)
    late = jnp.concatenate(
        [dot_nt(tall, top, HIGHEST), dot_nt(tall, bottom, HIGHEST)], axis=1
    )
    for index in range(dom_count):
        band = late[index * rows : (index + 1) * rows]
        late_parts[index, :rows] = band[:, :half]
        late_parts[index, rows : 2 * rows] = band[:, half:]
        last = late[half : half + 1, index * half : (index + 1) * half]
        late_parts[index, 2 * rows :] = last if index < 2 else jnp.zeros((1, half), F32)
    exchange(part_copy, 1, dom_count)
    finish(part_copy, 0, dom_count)
    mine[...] = jnp.sum(landed[...], axis=0) + parts[dom]
    exchange(line_copy, 0, col_count)
    finish(part_copy, 1, dom_count)
    late_mine[...] = jnp.sum(late_landed[...], axis=0) + late_parts[dom]
    exchange(line_copy, 1, col_count)
    finish(line_copy, 0, col_count)
    total[...] = jnp.sum(lines[...], axis=0) + mine[...]
    exchange(whole_copy, 0, dom_count)
    whole[dom] = total[...]
    finish(line_copy, 1, col_count)
    late_total[...] = jnp.sum(late_lines[...], axis=0) + late_mine[...]
    exchange(whole_copy, 1, dom_count)
    late_whole[dom] = late_total[...]
    finish(whole_copy, 0, dom_count)
    first = jnp.concatenate([whole[index] for index in range(dom_count)], axis=0)
    inverse_ref[...] = eliminate([first])[0]
    finish(whole_copy, 1, dom_count)
    gram_ref[...] = late_whole[...]

    @pl.loop(1, reach + 1)
    def _(o):
        for late in range(2):
            dom_copy(late, o).wait_send()

    @pl.loop(1, col_count)
    def _(o):
        for late in range(2):
            col_copy(late, o).wait_send()
            line_copy(late, o).wait_send()

    @pl.loop(1, dom_count)
    def _(o):
        for late in range(2):
            part_copy(late, o).wait_send()
            whole_copy(late, o).wait_send()


def tree_sum(terms):
    while len(terms) > 1:
        odd = [terms[-1]] if len(terms) % 2 else []
        terms = [a + b for a, b in zip(terms[::2], terms[1::2])] + odd
    return terms[0]


def split_three(x):
    high = x.astype(BF16)
    rest = x - high.astype(F32)
    middle = rest.astype(BF16)
    return high, middle, (rest - middle.astype(F32)).astype(BF16)


def product(a, b):
    ah, am, al = split_three(a)
    bh, bm, bl = split_three(b)

    def pair(a1, b1, a2, b2):
        return dot_nn(
            jnp.concatenate([a1, a2], axis=1), jnp.concatenate([b1, b2], axis=0)
        )

    return pair(ah, bh, am, bh) + (pair(ah, bm, am, bm) + pair(ah, bl, al, bh))


def eliminate(wide):
    size = wide[0].shape[0]
    shape = (PIVOTS, size)
    row, lane = iota(shape, 0), iota(shape, 1)
    blocks = [[w[k : k + PIVOTS] for w in wide] for k in range(0, size, PIVOTS)]

    def columns_of(block, start):
        return [
            jnp.broadcast_to(block[:, start + j : start + j + 1], shape) for j in range(PIVOTS)
        ]

    for turn, panel in enumerate(blocks):
        start = turn * PIVOTS
        inside = (lane >= start) & (lane < start + PIVOTS)
        columns = jnp.stack(columns_of(panel[0], start))
        first = jnp.where(inside, (lane - start == row).astype(F32), panel[0])
        work = jnp.stack([first] + panel[1:])
        scales = jnp.zeros(shape, F32)
        for i in range(PIVOTS):
            here = row == i
            column = columns[0]
            scale = 1.0 / jnp.broadcast_to(column[i : i + 1], shape)
            factor = jnp.where(here, 0.0, column * scale)
            scales = jnp.where(here, scale, scales)
            if i + 1 < PIVOTS:
                columns = columns[1:]
                columns = columns - factor * columns[:, i : i + 1]
            work = work - factor * work[:, i : i + 1]
        work = work * scales
        done = [work[w] for w in range(len(wide))]

        def kept(block):
            return [jnp.where(inside, 0.0, block[0])] + block[1:]

        ahead = None
        if turn + 1 < len(blocks):
            block = blocks[turn + 1]
            held = columns_of(block[0], start)
            ahead = [
                x - tree_sum([held[k] * done[w][k : k + 1] for k in range(PIVOTS)])
                for w, x in enumerate(kept(block))
            ]
        left = jnp.concatenate([jnp.where(inside, b[0], 0.0) for b in blocks], axis=0)
        empty = jnp.zeros((PIVOTS, size * len(wide)), F32)
        right = [empty] * len(blocks)
        right[turn] = jnp.concatenate(done, axis=1)
        change = product(left, jnp.concatenate(right, axis=0))
        for k, block in enumerate(blocks):
            if k == turn:
                blocks[k] = done
            elif k == turn + 1:
                blocks[k] = ahead
            else:
                rows = change[k * PIVOTS : (k + 1) * PIVOTS]
                blocks[k] = [
                    x - rows[:, size * w : size * (w + 1)] for w, x in enumerate(kept(block))
                ]
    return [jnp.concatenate([b[w] for b in blocks], axis=0) for w in range(len(wide))]


def solve_kernel(
    col_ref, gram_ref, inverse_ref, basis_ref, residual_ref, out_ref, basis_out_ref, residual_out_ref, sems
):
    copies = [
        pltpu.make_async_copy(basis_ref, basis_out_ref, sems.at[0]),
        pltpu.make_async_copy(residual_ref, residual_out_ref, sems.at[1]),
    ]
    for copy in copies:
        copy.start()
    dom_count, height, half = gram_ref.shape
    rows = half // dom_count
    bands = [gram_ref[k] for k in range(dom_count)]
    cross = jnp.concatenate([band[:rows] for band in bands], axis=0)
    second = jnp.concatenate([band[rows : 2 * rows] for band in bands], axis=0)
    gradient = jnp.concatenate([band[height - 1 :] for band in bands[:2]], axis=1)
    first_inverse = inverse_ref[...]
    carried = product(cross, first_inverse)
    second = second - dot_nt(carried, cross, HIGHEST)
    top = jnp.broadcast_to(gradient[:, :half], (8, half))
    x_top = dot_nn(top, first_inverse, HIGHEST)[:1]
    low = gradient[:, half:] - dot_nt(top, carried, HIGHEST)[:1]
    low = jnp.broadcast_to(low, (half, half)).T
    second_inverse, back = eliminate([second, -carried])
    x_bottom = jnp.sum(low * second_inverse, axis=0, keepdims=True)
    x_top = x_top + jnp.sum(low * back, axis=0, keepdims=True)
    width = out_ref.shape[1]
    out = jnp.zeros((1, width), F32)
    for index in range(2 * half // width):
        mine = slice(index * width // 2, (index + 1) * width // 2)
        own = -jnp.concatenate([x_top[:, mine], x_bottom[:, mine]], axis=1)
        out = jnp.where(col_ref[0] == index, own, out)
    out_ref[...] = out
    for copy in copies:
        copy.wait()


VMEM = pl.BlockSpec(memory_space=pltpu.VMEM)
SMEM = pl.BlockSpec(memory_space=pltpu.SMEM)
ANY = pl.BlockSpec(memory_space=pl.ANY)


def body(basis_panel, jacobian, neighbors, sample_rows, residual_parts):
    dom_count, col_count = lax.axis_size("dom"), lax.axis_size("col")
    col_index = lax.axis_index("col")
    width = basis_panel.shape[0]
    entries = sample_rows.shape[0]
    elements = neighbors.shape[0]
    node = jacobian.shape[1]
    size = width * col_count
    shape = jax.ShapeDtypeStruct
    reach = min(dom_count - 1, REACH_MOST)
    part = ROWS_DEV // col_count
    early = (size // 2 // dom_count, size // 2)
    chunk = (size // dom_count + 1, size // 2)
    jacobian_basis, sampled_residual, whole, inverse = pl.pallas_call(
        functools.partial(step_kernel, dom_count, col_count, reach),
        out_shape=(
            pltpu.VMEM((width, ROWS_DEV), F32), pltpu.VMEM((1, ROWS_DEV), F32), pltpu.VMEM((dom_count,) + chunk, F32), pltpu.VMEM((size // 2, size // 2), F32)
        ),
        in_specs=[ANY] * 5,
        out_specs=(VMEM, VMEM, VMEM, VMEM),
        scratch_shapes=[
            pltpu.SMEM(neighbors.shape[::-1], jnp.int32),
            pltpu.VMEM((1, entries), jnp.int32),
            pltpu.VMEM((1, entries), F32),
            pltpu.VMEM(basis_panel.shape, BF16),
            pltpu.VMEM(jacobian.shape, BF16),
            pltpu.SemaphoreType.DMA((3 + 2 * LOADS,)),
            pltpu.VMEM((elements, width, -(-node // LANES) * LANES), BF16),
            pltpu.VMEM((2 * width + 32, entries), BF16),
            pltpu.VMEM((reach, width // 2 + 2, CAP), F32),
            pltpu.VMEM((reach, width // 2, CAP), F32),
            pltpu.VMEM((reach, width // 2 + 2, CAP), F32),
            pltpu.VMEM((reach, width // 2, CAP), F32),
            pltpu.VMEM((width + 8, ROWS_DEV), F32),
            pltpu.VMEM((entries, LANES), BF16),
            pltpu.VMEM((entries, LANES), BF16),
            pltpu.VMEM((width + 32, reach * CAP), BF16),
            pltpu.VMEM((width, reach * CAP), BF16),
            pltpu.VMEM((1, reach * CAP), jnp.int32),
            pltpu.VMEM((2, col_count, width // 2, part), F32),
            pltpu.VMEM((2, col_count, width // 2, part), F32),
            pltpu.VMEM((dom_count,) + early, F32),
            pltpu.VMEM((dom_count - 1,) + early, F32),
            pltpu.VMEM(early, F32),
            pltpu.VMEM((col_count - 1,) + early, F32),
            pltpu.VMEM(early, F32),
            pltpu.VMEM((dom_count,) + early, F32),
            pltpu.VMEM((dom_count,) + chunk, F32),
            pltpu.VMEM((dom_count - 1,) + chunk, F32),
            pltpu.VMEM(chunk, F32),
            pltpu.VMEM((col_count - 1,) + chunk, F32),
            pltpu.VMEM(chunk, F32),
            pltpu.VMEM((dom_count,) + chunk, F32),
            pltpu.SemaphoreType.DMA((2, 2 * reach)),
            pltpu.SemaphoreType.DMA((2, 2 * (col_count - 1))),
            pltpu.SemaphoreType.DMA((2, 2 * (dom_count - 1))),
            pltpu.SemaphoreType.DMA((2, 2 * (col_count - 1))),
            pltpu.SemaphoreType.DMA((2, 2 * (dom_count - 1))),
        ],
        compiler_params=pltpu.CompilerParams(
            collective_id=0, has_side_effects=True, vmem_limit_bytes=VMEM_BYTES
        ),
        name="step",
    )(
        neighbors.T,
        basis_panel,
        jacobian,
        sample_rows.reshape(1, entries),
        residual_parts.reshape(1, entries),
    )
    reduced_step, jacobian_basis, sampled_residual = pl.pallas_call(
        solve_kernel,
        out_shape=(
            shape((1, width), F32), shape((width, ROWS_DEV), F32), shape((1, ROWS_DEV), F32)
        ),
        in_specs=[SMEM, VMEM, VMEM, VMEM, VMEM],
        out_specs=(VMEM, ANY, ANY),
        scratch_shapes=[pltpu.SemaphoreType.DMA((2,))],
        compiler_params=pltpu.CompilerParams(vmem_limit_bytes=VMEM_BYTES),
        name="solve",
    )(
        col_index.astype(jnp.int32).reshape(1),
        pltpu.with_memory_space_constraint(whole, pltpu.VMEM),
        pltpu.with_memory_space_constraint(inverse, pltpu.VMEM),
        pltpu.with_memory_space_constraint(jacobian_basis, pltpu.VMEM),
        pltpu.with_memory_space_constraint(sampled_residual, pltpu.VMEM),
    )
    return (jacobian_basis, sampled_residual[0], reduced_step[0])


def solution(mesh):
    placed = (P("col", "dom"), P(None, None, "dom"), P("dom", None), P("dom"), P("dom"))
    return jax.shard_map(
        body,
        mesh=mesh,
        in_specs=placed,
        out_specs=(P("col", "dom"), P("dom"), P("col")),
        check_vma=False,
    )
```

```python
import functools

import jax
import jax.numpy as jnp
from jax import lax
from jax.experimental import pallas as pl
from jax.experimental.pallas import tpu as pltpu
from jax.sharding import PartitionSpec as P

ROWS_DEV = 1024
CAP = 256
REACH_MOST = 8
LANES = 128
PIVOTS = 16
LOADS = 2
VMEM_BYTES = 62 * 2**20
HIGHEST = lax.Precision.HIGHEST
F32 = jnp.float32
BF16 = jnp.bfloat16


def iota(shape, dim):
    return lax.broadcasted_iota(jnp.int32, shape, dim)


def dot_nn(a, b, precision=None):
    return lax.dot_general(
        a, b, (((1,), (0,)), ((), ())), precision=precision, preferred_element_type=F32
    )


def dot_nt(a, b, precision=None):
    return lax.dot_general(
        a, b, (((1,), (1,)), ((), ())), precision=precision, preferred_element_type=F32
    )


def dot_tn(a, b, precision=None):
    return lax.dot_general(
        a, b, (((0,), (0,)), ((), ())), precision=precision, preferred_element_type=F32
    )


def split_values(x):
    high = x.astype(BF16)
    return high, (x - high.astype(F32)).astype(BF16)


def split_extra(x):
    high = x.astype(BF16).astype(F32)
    middle = (x - high).astype(BF16).astype(F32)
    low = x - high - middle
    return jnp.concatenate([high, middle, low, jnp.zeros_like(x)], axis=0).astype(BF16)


def join(found, width):
    values = found[:width] + found[width : 2 * width]
    base = 2 * width
    extra = found[base : base + 8] + found[base + 8 : base + 16] + found[base + 16 : base + 24]
    return jnp.concatenate([values, extra], axis=0)


def spread_places(places, height):
    turned = jnp.concatenate(
        [
            jnp.broadcast_to(places[:, k : k + LANES], (LANES, LANES)).T
            for k in range(0, height, LANES)
        ],
        axis=0,
    )
    tile = turned >> (CAP.bit_length() - 1)
    return tile.astype(F32).astype(BF16), (turned & (CAP - 1)).astype(F32).astype(BF16)


def pick(terms, tiles, spots, tile):
    wanted = jnp.asarray(tile, jnp.int32).astype(F32)
    near = jnp.where(tiles == jnp.full(tiles.shape, wanted, F32).astype(BF16), spots, -1.0)
    lanes = [
        (iota(tiles.shape, 1) + start).astype(F32).astype(BF16) for start in range(0, CAP, LANES)
    ]
    chosen = jnp.concatenate([jnp.where(near == lane, 1.0, 0.0) for lane in lanes], axis=1)
    return dot_nn(terms, chosen.astype(BF16))


def pick_turned(terms, targets, base):
    count = targets.shape[1]
    near = jnp.clip(targets - base, -1, CAP).astype(F32)
    near = jnp.broadcast_to(near, (16, count)).astype(BF16)
    near = jnp.concatenate([near] * (CAP // 16), axis=0)
    spots = iota((CAP, LANES), 0).astype(F32).astype(BF16)
    spots = jnp.concatenate([spots] * (count // LANES), axis=1)
    return dot_nt(terms, jnp.where(spots == near, 1.0, 0.0).astype(BF16))


def fold(value, count):
    return jnp.where(value >= count, value - count, value)


def step_kernel(
    dom_count, col_count, reach,
    links_hbm, panel_hbm, blocks_hbm, rows_hbm, parts_hbm,
    basis_ref, residual_ref, gram_ref, inverse_ref,
    links_ref, rows_ref, parts_ref, panel_ref, blocks_ref, load_sems, panels, terms,
    send, send_late, arrived, arrived_late, local, tiles_held, spots_held,
    terms_in, terms_late, landing, pieces, others,
    parts, landed, mine, lines, total, whole,
    late_parts, late_landed, late_mine, late_lines, late_total, late_whole,
    dom_sems, col_sems, part_sems, line_sems, whole_sems,
):
    dom, col = lax.axis_index("dom"), lax.axis_index("col")
    width = panel_ref.shape[0]
    coupled_count, node, entries = blocks_ref.shape
    elements = links_ref.shape[1]
    rs = entries // elements
    group = LANES // rs
    part = ROWS_DEV // col_count
    size = width * col_count
    half_width = width // 2

    def remote(source, target, sems, index, device):
        return pltpu.make_async_remote_copy(
            src_ref=source,
            dst_ref=target,
            send_sem=sems.at[0, index],
            recv_sem=sems.at[1, index],
            device_id=device,
            device_id_type=pl.DeviceIdType.MESH,
        )

    def dom_at(o):
        return fold(dom + o, dom_count), col

    def col_at(o):
        return dom, fold(col + o, col_count)

    def offset_at(turn):
        if reach != dom_count - 1 or dom_count & reach:
            return turn + 1
        flips = jnp.where(turn < reach - 1, reach - 1 - turn // 2 * 2 + turn % 2, 1)
        partner, bit = 0, 1
        while bit < dom_count:
            partner = partner + (dom // bit + flips // bit) % 2 * bit
            bit *= 2
        return (dom_count + partner - dom) % dom_count

    def dom_copy(half, o):
        source, target = ((send, arrived), (send_late, arrived_late))[half]
        return remote(source.at[o - 1], target.at[o - 1], dom_sems, half * reach + o - 1, dom_at(o))

    def col_copy(half, o):
        there = fold(col + o, col_count)
        return remote(
            pieces.at[half, there], others.at[half, col],
            col_sems, half * (col_count - 1) + o - 1, col_at(o),
        )

    def part_copy(late, o):
        source, target = ((parts, landed), (late_parts, late_landed))[late]
        place = late * (dom_count - 1) + o - 1
        there = fold(dom + o, dom_count)
        return remote(source.at[there], target.at[o - 1], part_sems, place, dom_at(o))

    def line_copy(late, o):
        source, target = ((mine, lines), (late_mine, late_lines))[late]
        place = late * (col_count - 1) + o - 1
        return remote(source, target.at[o - 1], line_sems, place, col_at(o))

    def whole_copy(late, o):
        source, target = ((total, whole), (late_total, late_whole))[late]
        place = late * (dom_count - 1) + o - 1
        return remote(source, target.at[dom], whole_sems, place, dom_at(o))

    def panel_load(k):
        share = elements // LOADS * node
        place = slice(k * share, (k + 1) * share)
        return pltpu.make_async_copy(
            panel_hbm.at[:, place], panel_ref.at[:, place], load_sems.at[3 + k]
        )

    def blocks_load(k):
        share = entries // LOADS
        place = slice(k * share, (k + 1) * share)
        return pltpu.make_async_copy(
            blocks_hbm.at[:, :, place], blocks_ref.at[:, :, place], load_sems.at[3 + LOADS + k]
        )

    small_loads = [
        pltpu.make_async_copy(rows_hbm, rows_ref, load_sems.at[0]),
        pltpu.make_async_copy(parts_hbm, parts_ref, load_sems.at[1]),
        pltpu.make_async_copy(links_hbm, links_ref, load_sems.at[2]),
    ]
    for load in small_loads:
        load.start()
    for k in range(LOADS):
        panel_load(k).start()
    for k in range(LOADS):
        blocks_load(k).start()
    barrier = pltpu.get_barrier_semaphore()

    for count, device_at in ((dom_count, dom_at), (col_count, col_at)):

        @pl.loop(1, count)
        def _(o, device_at=device_at):
            pl.semaphore_signal(
                barrier, inc=1, device_id=device_at(o), device_id_type=pl.DeviceIdType.MESH
            )

    for load in small_loads:
        load.wait()
    shift = ROWS_DEV.bit_length() - 1
    match_rows = max(16, dom_count)
    before = (iota((LANES, LANES), 0) < iota((LANES, LANES), 1)).astype(F32).astype(BF16)
    carry = jnp.zeros((match_rows, 1), F32)
    targets = []
    for start in range(0, entries, LANES):
        rows = rows_ref[:, start : start + LANES]
        offset = fold((rows >> shift) - dom + dom_count, dom_count)
        local_row = rows & (ROWS_DEV - 1)
        matches = (iota((match_rows, LANES), 0) == offset).astype(F32)
        ranks = jnp.sum(
            matches * (dot_nn(matches.astype(BF16), before) + carry), axis=0, keepdims=True
        ).astype(jnp.int32)
        carry = carry + jnp.sum(matches, axis=1, keepdims=True)
        targets.append(
            jnp.where(offset == 0, local_row, ROWS_DEV + (offset - 1) * CAP + ranks)
        )
    targets = jnp.concatenate(targets, axis=1)
    tiles_held[...], spots_held[...] = spread_places(targets, entries)

    row_values = (rows_ref[...] & (ROWS_DEV - 1)).astype(F32)
    which = iota((8, entries), 0)
    extra = jnp.where(which == 0, parts_ref[...], jnp.where(which == 1, row_values, 0.0))
    terms[2 * width :, :] = split_extra(extra)

    deep = panels.shape[2]
    no_columns = jnp.zeros((width, deep - node), BF16)
    no_rows = jnp.zeros((deep - node, LANES), BF16)
    pairs = elements // 2 // LOADS
    for k in range(LOADS):
        panel_load(k).wait()

        @pl.loop(k * pairs, (k + 1) * pairs, unroll=8)
        def _(pair):
            window = panel_ref[:, pl.ds(pl.multiple_of(pair * 2 * node, LANES), 2 * node)]
            for which in range(2):
                held = window[:, which * node : (which + 1) * node]
                panels[2 * pair + which] = jnp.concatenate([held, no_columns], axis=1)

    lane_element = iota((width, LANES), 1) // rs

    shares = elements // group // LOADS
    for k in range(LOADS):
        blocks_load(k).wait()

        @pl.loop(k * shares, (k + 1) * shares, unroll=shares)
        def _(block):
            columns = pl.ds(pl.multiple_of(block * LANES, LANES), LANES)
            picked = jnp.concatenate(
                [
                    jnp.concatenate(
                        [panels[links_ref[coupled, block * group + q]] for q in range(group)], axis=0
                    )
                    for coupled in range(coupled_count)
                ],
                axis=1,
            )
            against = []
            for coupled in range(coupled_count):
                against += [blocks_ref[coupled, :, columns], no_rows]
            found = dot_nn(picked, jnp.concatenate(against, axis=0))
            out = found[:width]
            for q in range(1, group):
                out = jnp.where(lane_element == q, found[q * width : (q + 1) * width], out)
            high, low = split_values(out)
            terms[:width, columns] = high
            terms[width : 2 * width, columns] = low

    pl.semaphore_wait(barrier, dom_count + col_count - 2)

    @pl.loop(0, reach)
    def _(turn):
        o = offset_at(turn)
        found = join(pick(terms[...], tiles_held[...], spots_held[...], ROWS_DEV // CAP + o - 1), width)
        send[o - 1, :half_width] = found[:half_width]
        send[o - 1, half_width:] = found[width : width + 2]
        send_late[o - 1] = found[half_width:width]
        dom_copy(0, o).start()

    @pl.loop(0, reach)
    def _(turn):
        dom_copy(1, offset_at(turn)).start()

    @pl.loop(0, ROWS_DEV // CAP)
    def _(tile):
        base = tile * CAP
        local[:, pl.ds(pl.multiple_of(base, CAP), CAP)] = join(
            pick(terms[...], tiles_held[...], spots_held[...], tile), width
        )

    def assemble(half, base):
        columns = pl.ds(pl.multiple_of(base, CAP), CAP)
        found = pick_turned((terms_in, terms_late)[half][...], landing[...], base)
        start = half * half_width
        values = found[:half_width] + found[half_width : 2 * half_width]
        values = values + local[start : start + half_width, columns]
        basis_ref[start : start + half_width, columns] = values
        if half == 0:
            extra = found[2 * half_width :]
            extra = extra[:8] + extra[8:16] + extra[16:24] + local[width:, columns]
            residual_ref[:, columns] = extra[:1]
        return values

    def pass_on(half):
        if part == CAP:

            @pl.loop(1, col_count)
            def _(o):
                there = fold(col + o, col_count)
                pieces[half, there] = assemble(half, there * part)
                col_copy(half, o).start()

            others[half, col] = assemble(half, col * part)
            return
        for tile in range(ROWS_DEV // CAP):
            assemble(half, tile * CAP)
        rows = slice(half * half_width, (half + 1) * half_width)
        for index in range(col_count):
            pieces[half, index] = basis_ref[rows, index * part : (index + 1) * part]

        @pl.loop(1, col_count)
        def _(o):
            col_copy(half, o).start()

        others[half, col] = pieces[half, col]

    for o in range(1, reach + 1):
        dom_copy(0, o).wait_recv()
        columns = slice((o - 1) * CAP, o * CAP)
        block = arrived[o - 1]
        extra = jnp.concatenate([block[half_width:], jnp.zeros((6, CAP), F32)], axis=0)
        high, low = split_values(block[:half_width])
        terms_in[:, columns] = jnp.concatenate([high, low, split_extra(extra)], axis=0)
        landing[:, columns] = extra[1:2].astype(jnp.int32)

    pass_on(0)
    own_residual = jnp.zeros((1, part), F32)
    for index in range(col_count):
        piece = residual_ref[:, index * part : (index + 1) * part]
        own_residual = own_residual + jnp.where(index == col, piece, 0.0)

    for o in range(1, reach + 1):
        dom_copy(1, o).wait_recv()
        high, low = split_values(arrived_late[o - 1])
        terms_late[:, (o - 1) * CAP : o * CAP] = jnp.concatenate([high, low], axis=0)

    pass_on(1)
    half = size // 2
    rows = half // dom_count

    def exchange(copy, late, count):
        @pl.loop(0, count - 1, unroll=count - 1 if count < 16 else 1)
        def _(turn):
            copy(late, offset_at(turn) if count == dom_count else turn + 1).start()

    def finish(copy, late, count):
        @pl.loop(1, count)
        def _(o):
            copy(late, o).wait_recv()

    for o in range(1, col_count):
        col_copy(0, o).wait_recv()
    top = others[0].reshape(half, part)
    first = product(top, top, True)
    for index in range(dom_count):
        parts[index] = first[index * rows : (index + 1) * rows]
    exchange(part_copy, 0, dom_count)
    for o in range(1, col_count):
        col_copy(1, o).wait_recv()
    bottom = others[1].reshape(half, part)
    tall = jnp.concatenate([bottom, jnp.broadcast_to(own_residual, (8, part))], axis=0)
    late = jnp.concatenate(
        [product(tall, top, True), product(tall, bottom, True)], axis=1
    )
    for index in range(dom_count):
        band = late[index * rows : (index + 1) * rows]
        late_parts[index, :rows] = band[:, :half]
        late_parts[index, rows : 2 * rows] = band[:, half:]
        last = late[half : half + 1, index * half : (index + 1) * half]
        late_parts[index, 2 * rows :] = last if index < 2 else jnp.zeros((1, half), F32)
    exchange(part_copy, 1, dom_count)
    finish(part_copy, 0, dom_count)
    mine[...] = jnp.sum(landed[...], axis=0) + parts[dom]
    exchange(line_copy, 0, col_count)
    finish(part_copy, 1, dom_count)
    late_mine[...] = jnp.sum(late_landed[...], axis=0) + late_parts[dom]
    exchange(line_copy, 1, col_count)
    finish(line_copy, 0, col_count)
    total[...] = jnp.sum(lines[...], axis=0) + mine[...]
    exchange(whole_copy, 0, dom_count)
    whole[dom] = total[...]
    finish(line_copy, 1, col_count)
    late_total[...] = jnp.sum(late_lines[...], axis=0) + late_mine[...]
    exchange(whole_copy, 1, dom_count)
    late_whole[dom] = late_total[...]
    finish(whole_copy, 0, dom_count)
    first = jnp.concatenate([whole[index] for index in range(dom_count)], axis=0)
    inverse_ref[...] = eliminate([first])[0]

    @pl.loop(1, reach + 1)
    def _(o):
        for late in range(2):
            dom_copy(late, o).wait_send()

    @pl.loop(1, col_count)
    def _(o):
        for late in range(2):
            col_copy(late, o).wait_send()
            line_copy(late, o).wait_send()

    @pl.loop(1, dom_count)
    def _(o):
        for late in range(2):
            part_copy(late, o).wait_send()
        whole_copy(0, o).wait_send()

    finish(whole_copy, 1, dom_count)
    gram_ref[...] = late_whole[...]

    @pl.loop(1, dom_count)
    def _(o):
        whole_copy(1, o).wait_send()


def tree_sum(terms):
    while len(terms) > 1:
        odd = [terms[-1]] if len(terms) % 2 else []
        terms = [a + b for a, b in zip(terms[::2], terms[1::2])] + odd
    return terms[0]


def split_three(x):
    high = x.astype(BF16)
    rest = x - high.astype(F32)
    middle = rest.astype(BF16)
    return high, middle, (rest - middle.astype(F32)).astype(BF16)


def product(a, b, turned=False):
    ah, am, al = split_three(a)
    bh, bm, bl = split_three(b)

    def pair(a1, b1, a2, b2):
        left = jnp.concatenate([a1, a2], axis=1)
        if turned:
            return dot_nt(left, jnp.concatenate([b1, b2], axis=1))
        return dot_nn(left, jnp.concatenate([b1, b2], axis=0))

    return pair(ah, bh, am, bh) + (pair(ah, bm, am, bm) + pair(ah, bl, al, bh))


def eliminate(wide):
    size = wide[0].shape[0]
    shape = (PIVOTS, size)
    row, lane = iota(shape, 0), iota(shape, 1)
    blocks = [[w[k : k + PIVOTS] for w in wide] for k in range(0, size, PIVOTS)]

    def columns_of(block, start):
        return [
            jnp.broadcast_to(block[:, start + j : start + j + 1], shape) for j in range(PIVOTS)
        ]

    for turn, panel in enumerate(blocks):
        start = turn * PIVOTS
        inside = (lane >= start) & (lane < start + PIVOTS)
        columns = jnp.stack(columns_of(panel[0], start))
        first = jnp.where(inside, (lane - start == row).astype(F32), panel[0])
        work = jnp.stack([first] + panel[1:])
        scales = jnp.zeros(shape, F32)
        for i in range(PIVOTS):
            here = row == i
            column = columns[0]
            scale = 1.0 / jnp.broadcast_to(column[i : i + 1], shape)
            factor = jnp.where(here, 0.0, column * scale)
            scales = jnp.where(here, scale, scales)
            if i + 1 < PIVOTS:
                columns = columns[1:]
                columns = columns - factor * columns[:, i : i + 1]
            work = work - factor * work[:, i : i + 1]
        work = work * scales
        done = [work[w] for w in range(len(wide))]

        def kept(block):
            return [jnp.where(inside, 0.0, block[0])] + block[1:]

        ahead = None
        if turn + 1 < len(blocks):
            block = blocks[turn + 1]
            held = columns_of(block[0], start)
            ahead = [
                x - tree_sum([held[k] * done[w][k : k + 1] for k in range(PIVOTS)])
                for w, x in enumerate(kept(block))
            ]
        left = jnp.concatenate([jnp.where(inside, b[0], 0.0) for b in blocks], axis=0)
        empty = jnp.zeros((PIVOTS, size * len(wide)), F32)
        right = [empty] * len(blocks)
        right[turn] = jnp.concatenate(done, axis=1)
        change = product(left, jnp.concatenate(right, axis=0))
        for k, block in enumerate(blocks):
            if k == turn:
                blocks[k] = done
            elif k == turn + 1:
                blocks[k] = ahead
            else:
                rows = change[k * PIVOTS : (k + 1) * PIVOTS]
                blocks[k] = [
                    x - rows[:, size * w : size * (w + 1)] for w, x in enumerate(kept(block))
                ]
    return [jnp.concatenate([b[w] for b in blocks], axis=0) for w in range(len(wide))]


def solve_kernel(
    gram_ref, inverse_ref, basis_ref, residual_ref, out_ref, basis_out_ref, residual_out_ref, sems
):
    copies = [
        pltpu.make_async_copy(basis_ref, basis_out_ref, sems.at[0]),
        pltpu.make_async_copy(residual_ref, residual_out_ref, sems.at[1]),
    ]
    for copy in copies:
        copy.start()
    dom_count, height, half = gram_ref.shape
    rows = half // dom_count
    bands = [gram_ref[k] for k in range(dom_count)]
    cross = jnp.concatenate([band[:rows] for band in bands], axis=0)
    second = jnp.concatenate([band[rows : 2 * rows] for band in bands], axis=0)
    gradient = jnp.concatenate([band[height - 1 :] for band in bands[:2]], axis=1)
    first_inverse = inverse_ref[...]
    carried = product(cross, first_inverse)
    second = second - product(carried, cross, True)
    top = jnp.broadcast_to(gradient[:, :half], (8, half))
    x_top = dot_nn(top, first_inverse, HIGHEST)[:1]
    low = gradient[:, half:] - dot_nt(top, carried, HIGHEST)[:1]
    low = jnp.broadcast_to(low, (half, half)).T
    second_inverse, back = eliminate([second, -carried])
    x_bottom = jnp.sum(low * second_inverse, axis=0, keepdims=True)
    x_top = x_top + jnp.sum(low * back, axis=0, keepdims=True)
    width = out_ref.shape[1]
    out = jnp.zeros((1, width), F32)
    col = lax.axis_index("col")
    for index in range(2 * half // width):
        mine = slice(index * width // 2, (index + 1) * width // 2)
        own = -jnp.concatenate([x_top[:, mine], x_bottom[:, mine]], axis=1)
        out = jnp.where(col == index, own, out)
    out_ref[...] = out
    for copy in copies:
        copy.wait()


VMEM = pl.BlockSpec(memory_space=pltpu.VMEM)
ANY = pl.BlockSpec(memory_space=pl.ANY)


def body(basis_panel, jacobian, neighbors, sample_rows, residual_parts):
    dom_count, col_count = lax.axis_size("dom"), lax.axis_size("col")
    width = basis_panel.shape[0]
    entries = sample_rows.shape[0]
    elements = neighbors.shape[0]
    node = jacobian.shape[1]
    size = width * col_count
    shape = jax.ShapeDtypeStruct
    reach = min(dom_count - 1, REACH_MOST)
    part = ROWS_DEV // col_count
    early = (size // 2 // dom_count, size // 2)
    chunk = (size // dom_count + 1, size // 2)
    jacobian_basis, sampled_residual, whole, inverse = pl.pallas_call(
        functools.partial(step_kernel, dom_count, col_count, reach),
        out_shape=(
            pltpu.VMEM((width, ROWS_DEV), F32), pltpu.VMEM((1, ROWS_DEV), F32), pltpu.VMEM((dom_count,) + chunk, F32), pltpu.VMEM((size // 2, size // 2), F32)
        ),
        in_specs=[ANY] * 5,
        out_specs=(VMEM, VMEM, VMEM, VMEM),
        scratch_shapes=[
            pltpu.SMEM(neighbors.shape[::-1], jnp.int32),
            pltpu.VMEM((1, entries), jnp.int32),
            pltpu.VMEM((1, entries), F32),
            pltpu.VMEM(basis_panel.shape, BF16),
            pltpu.VMEM(jacobian.shape, BF16),
            pltpu.SemaphoreType.DMA((3 + 2 * LOADS,)),
            pltpu.VMEM((elements, width, -(-node // LANES) * LANES), BF16),
            pltpu.VMEM((2 * width + 32, entries), BF16),
            pltpu.VMEM((reach, width // 2 + 2, CAP), F32),
            pltpu.VMEM((reach, width // 2, CAP), F32),
            pltpu.VMEM((reach, width // 2 + 2, CAP), F32),
            pltpu.VMEM((reach, width // 2, CAP), F32),
            pltpu.VMEM((width + 8, ROWS_DEV), F32),
            pltpu.VMEM((entries, LANES), BF16),
            pltpu.VMEM((entries, LANES), BF16),
            pltpu.VMEM((width + 32, reach * CAP), BF16),
            pltpu.VMEM((width, reach * CAP), BF16),
            pltpu.VMEM((1, reach * CAP), jnp.int32),
            pltpu.VMEM((2, col_count, width // 2, part), F32),
            pltpu.VMEM((2, col_count, width // 2, part), F32),
            pltpu.VMEM((dom_count,) + early, F32),
            pltpu.VMEM((dom_count - 1,) + early, F32),
            pltpu.VMEM(early, F32),
            pltpu.VMEM((col_count - 1,) + early, F32),
            pltpu.VMEM(early, F32),
            pltpu.VMEM((dom_count,) + early, F32),
            pltpu.VMEM((dom_count,) + chunk, F32),
            pltpu.VMEM((dom_count - 1,) + chunk, F32),
            pltpu.VMEM(chunk, F32),
            pltpu.VMEM((col_count - 1,) + chunk, F32),
            pltpu.VMEM(chunk, F32),
            pltpu.VMEM((dom_count,) + chunk, F32),
            pltpu.SemaphoreType.DMA((2, 2 * reach)),
            pltpu.SemaphoreType.DMA((2, 2 * (col_count - 1))),
            pltpu.SemaphoreType.DMA((2, 2 * (dom_count - 1))),
            pltpu.SemaphoreType.DMA((2, 2 * (col_count - 1))),
            pltpu.SemaphoreType.DMA((2, 2 * (dom_count - 1))),
        ],
        compiler_params=pltpu.CompilerParams(
            collective_id=0, has_side_effects=True, vmem_limit_bytes=VMEM_BYTES
        ),
        name="step",
    )(
        neighbors.T,
        basis_panel,
        jacobian,
        sample_rows.reshape(1, entries),
        residual_parts.reshape(1, entries),
    )
    reduced_step, jacobian_basis, sampled_residual = pl.pallas_call(
        solve_kernel,
        out_shape=(
            shape((1, width), F32), shape((width, ROWS_DEV), F32), shape((1, ROWS_DEV), F32)
        ),
        in_specs=[VMEM, VMEM, VMEM, VMEM],
        out_specs=(VMEM, ANY, ANY),
        scratch_shapes=[pltpu.SemaphoreType.DMA((2,))],
        compiler_params=pltpu.CompilerParams(vmem_limit_bytes=VMEM_BYTES),
        name="solve",
    )(
        pltpu.with_memory_space_constraint(whole, pltpu.VMEM),
        pltpu.with_memory_space_constraint(inverse, pltpu.VMEM),
        pltpu.with_memory_space_constraint(jacobian_basis, pltpu.VMEM),
        pltpu.with_memory_space_constraint(sampled_residual, pltpu.VMEM),
    )
    return (jacobian_basis, sampled_residual[0], reduced_step[0])


def solution(mesh):
    placed = (P("col", "dom"), P(None, None, "dom"), P("dom", None), P("dom"), P("dom"))
    return jax.shard_map(
        body,
        mesh=mesh,
        in_specs=placed,
        out_specs=(P("col", "dom"), P("dom"), P("col")),
        check_vma=False,
    )
```
